32 devices in a mesh: mem: 4 (over y, core), lat: 4 (over z), lon: 2 (over x).
Axes of the slice: x: 2, y: 2, z: 4, core: 2. Of those that a mesh axis runs over, the one named last changes fastest.
Arguments:
- perturbations: bfloat16 [4, 8, 128, 256], P('mem', None, 'lat', 'lon'), may hold values from -6 to 6
- control: float32 [4, 8, 128, 256], P('mem', None, 'lat', 'lon'), may hold values from -6 to 6
- diffusivity: float32 [8, 128, 256], P(None, 'lat', 'lon'), may hold values from 0.03 to 0.24
- obs_cells: int32 [32, 512], P(('mem', 'lat', 'lon')), may hold values from 0 to 8191
- obs_counts: int32 [32], P(('mem', 'lat', 'lon')), may hold values from 256 to 512, as said below
- innovations: float32 [32, 512], P(('mem', 'lat', 'lon')), may hold values from -8 to 8
- obs_precision: float32 [32, 512], P(('mem', 'lat', 'lon')), may hold values from 0.5 to 2
Outputs:
- analysis_control: float32 [4, 8, 128, 256], P('mem', None, 'lat', 'lon')
The draws below stay inside these ranges and needn't reach their ends.
Inputs may be any that keep to these rules, and one draw needn't show every extreme that they name: `obs_cells`: an entry names a cell of its own tile, counted as level times 8 * 128 plus tile row times 128 plus tile column; one cell may be named by several slots. `obs_counts`: slots at and beyond a tile's count are ignored; in every draw some tile is full.
All inputs are finite; a program needn't handle non-finite values.
Results may differ from the reference program's by a relative error of at most 0.0003.
Values sent between devices are 32-bit elements; how exact they have to be, the bound alone decides.
A program may use at most 64 MiB of HBM per device.

```python
import math
import jax
import jax.numpy as jnp
from jax import lax

LEV = 8
LAT_DEV = 32
LON_DEV = 128
OBS_TILE = 512
SWEEPS = 4
STEPS = 2
MEMBERS = 4
NLAT = 128
NLON = 256
ROWS_TILE = 8
TILE_CELLS = 8192
TILES = 32
N_LAT = 4
N_LON = 2


def draw_obs_counts(key, part):
    count_key, pick_key = jax.random.split(jax.random.fold_in(key, 11))
    counts = jax.random.randint(count_key, (TILES,), OBS_TILE // 2, OBS_TILE + 1)
    chosen = jax.random.randint(pick_key, (), 0, TILES)
    return jnp.where(jnp.arange(TILES) == chosen, OBS_TILE, counts).astype(jnp.int32)


def place_ends(drawn, key, smallest, high):
    spot = [jax.random.randint(jax.random.fold_in(key, axis), (), 0, length) for axis, length in enumerate(drawn.shape)]
    main_axis = drawn.shape.index(max(drawn.shape))
    neighbour = spot[:main_axis] + [(spot[main_axis] + 1) % drawn.shape[main_axis]] + spot[main_axis + 1:]
    return drawn.at[tuple(spot)].set(smallest).at[tuple(neighbour)].set(high)


def shard_levels(key, shape, shards, least, largest):
    def one(position, parts):
        heights = jax.random.uniform(jax.random.fold_in(jax.random.fold_in(key, 6), position), (parts,), jnp.float32, least / len(shards), largest / len(shards))
        return jnp.repeat(jnp.exp(heights), shape[position] // parts).reshape((-1,) + (1,) * (len(shape) - position - 1))

    level = one(*shards[0])
    for cut in shards[1:]:
        level = level * one(*cut)
    return level


def bell_draw(stream_key, dims, scale, bound, shards=(), held_as=jnp.bfloat16):
    drawn = jax.random.normal(stream_key, dims, jnp.float32) * scale
    if len(shards) > 0:
        drawn = shard_levels(stream_key, dims, shards, -0.22, 0.18) * drawn
    return jnp.clip(drawn, min=-bound, max=bound).astype(held_as)


def setup_inputs(seed: int = 0) -> dict:
    key_of = jax.random.split(jax.random.key(seed), 8)
    return {
        "perturbations": bell_draw(key_of[0], (MEMBERS, LEV, NLAT, NLON), 1.0, 6.0, ((0, 4), (2, 4), (3, 2))),
        "control": bell_draw(key_of[1], (MEMBERS, LEV, NLAT, NLON), 1.0, 6.0, ((0, 4), (2, 4), (3, 2)), jnp.float32),
        "diffusivity": jnp.clip(jnp.exp(math.log(0.24) - 2.0794415 * jax.random.uniform(key_of[2], (LEV, NLAT, NLON), jnp.float32) ** shard_levels(key_of[2], (LEV, NLAT, NLON), ((1, 4), (2, 2)), -0.2, 0.2)), 0.03, 0.24),
        "obs_cells": place_ends(jax.random.randint(key_of[3], (TILES, OBS_TILE), 0, TILE_CELLS), jax.random.fold_in(key_of[3], 1), 0, TILE_CELLS - 1).astype(jnp.int32),
        "obs_counts": draw_obs_counts(jax.random.fold_in(key_of[7], 71), 0),
        "innovations": bell_draw(key_of[5], (TILES, OBS_TILE), 1.5, 8.0, ((0, 32),), jnp.float32),
        "obs_precision": jnp.clip(jnp.exp(math.log(2.0) - 1.3862944 * jax.random.uniform(key_of[6], (TILES, OBS_TILE), jnp.float32) ** shard_levels(key_of[6], (TILES, OBS_TILE), ((0, 32),), -0.2, 0.2)), 0.5, 2.0),
    }


huber_edge = 1.5
step_length = 0.5

def laplacian(state_field):
    padded = jnp.pad(state_field, ((0, 0), (1, 1), (0, 0)))
    return padded[:, :-2, :] + padded[:, 2:, :] + jnp.roll(state_field, 1, axis=2) + jnp.roll(state_field, -1, axis=2) - 4.0 * state_field

def smooth(state_field, diffusivity):
    for sweep_index in range(SWEEPS):
        state_field = state_field + diffusivity * laplacian(state_field)
    return state_field

def adjoint(state_field, diffusivity):
    for sweep_index in range(SWEEPS):
        state_field = state_field + laplacian(diffusivity * state_field)
    return state_field

def flat_positions(obs_cells):
    tile_ids = jnp.arange(TILES, dtype=jnp.int32)
    member_part = tile_ids // (N_LAT * N_LON)
    lat_part = tile_ids // N_LON % N_LAT
    lon_part = tile_ids % N_LON
    level_index = obs_cells // (ROWS_TILE * LON_DEV)
    tile_row = obs_cells // LON_DEV % ROWS_TILE
    tile_column = obs_cells % LON_DEV
    global_row = lat_part[:, None] * LAT_DEV + member_part[:, None] * ROWS_TILE + tile_row
    global_column = lon_part[:, None] * LON_DEV + tile_column
    return ((level_index * NLAT + global_row) * NLON + global_column).astype(jnp.int32)

def reference(perturbations, control, diffusivity, obs_cells, obs_counts, innovations, obs_precision):
    weight = 1.0 / math.sqrt(MEMBERS - 1)
    positions = flat_positions(obs_cells).reshape(-1)
    live_slots = (jnp.arange(OBS_TILE, dtype=jnp.int32)[None, :] < obs_counts[:, None]).astype(jnp.float32)
    alpha_all = control
    for step_index in range(STEPS):

        def accumulate(member_total, member_pair):
            member_x, member_alpha = member_pair
            return (member_total + member_x.astype(jnp.float32) * smooth(member_alpha, diffusivity), None)
        member_total, unused = lax.scan(accumulate, jnp.zeros((LEV, NLAT, NLON), jnp.float32), (perturbations, alpha_all))
        increment = weight * member_total
        observed = increment.reshape(-1)[positions].reshape(obs_cells.shape)
        misfit = (observed - innovations) * obs_precision
        pulled = jnp.clip(misfit, -huber_edge, huber_edge) * obs_precision * live_slots
        forcing = jnp.zeros((LEV * NLAT * NLON,), jnp.float32).at[positions].add(pulled.reshape(-1)).reshape(LEV, NLAT, NLON)

        def update(member_pair):
            member_x, member_alpha = member_pair
            gradient = member_alpha + adjoint(weight * member_x.astype(jnp.float32) * forcing, diffusivity)
            return member_alpha - step_length * gradient
        alpha_all = lax.map(update, (perturbations, alpha_all))
    return alpha_all
```

```python
import functools
import math

import jax
import jax.numpy as jnp
from jax import lax
from jax.experimental import pallas as pl
from jax.experimental.pallas import tpu as pltpu
from jax.sharding import PartitionSpec as P

SWEEPS = 4
STEPS = 2


huber_edge = 1.5
step_length = 0.5


def with_halo(cells, sides, width):
    for axis, dim in sides:
        count = lax.axis_size(axis)
        head = lax.slice_in_dim(cells, 0, width, axis=dim)
        tail = lax.slice_in_dim(cells, cells.shape[dim] - width, cells.shape[dim], axis=dim)
        cells = jnp.concatenate(
            [
                lax.ppermute(tail, axis, [(i, (i + 1) % count) for i in range(count)]),
                cells,
                lax.ppermute(head, axis, [((i + 1) % count, i) for i in range(count)]),
            ],
            axis=dim,
        )
    return cells


def inside_rows(lat_rows, margin):
    first_row = lax.axis_index("lat") * lat_rows - margin
    global_rows = first_row + jnp.arange(lat_rows + 2 * margin, dtype=jnp.int32)
    total_rows = lat_rows * lax.axis_size("lat")
    return ((global_rows >= 0) & (global_rows < total_rows)).astype(jnp.float32)[None, :, None]


def stencil(padded):
    center = padded[:, 1:-1, 1:-1]
    laplace_term = (
        padded[:, :-2, 1:-1]
        + padded[:, 2:, 1:-1]
        + padded[:, 1:-1, :-2]
        + padded[:, 1:-1, 2:]
        - 4.0 * center
    )
    return (laplace_term, center)


def smooth_deep(state_field, kappa_rim):
    lat_rows = state_field.shape[1]
    padded = with_halo(state_field, (("lat", 1), ("lon", 2)), SWEEPS)
    padded = padded * inside_rows(lat_rows, SWEEPS)
    for sweep_index in range(SWEEPS):
        offset = sweep_index + 1
        local_kappa = kappa_rim[
            :, offset : kappa_rim.shape[1] - offset, offset : kappa_rim.shape[2] - offset
        ]
        laplace_term, center = stencil(padded)
        padded = (center + local_kappa * laplace_term) * inside_rows(lat_rows, SWEEPS - offset)
    return padded


def adjoint_deep(state_field, kappa_rim):
    lat_rows = state_field.shape[1]
    padded = with_halo(state_field, (("lat", 1), ("lon", 2)), SWEEPS)
    padded = padded * inside_rows(lat_rows, SWEEPS)
    for sweep_index in range(SWEEPS):
        local_kappa = kappa_rim[
            :,
            sweep_index : kappa_rim.shape[1] - sweep_index,
            sweep_index : kappa_rim.shape[2] - sweep_index,
        ]
        laplace_term, center = stencil(local_kappa * padded)
        padded = (padded[:, 1:-1, 1:-1] + laplace_term) * inside_rows(
            lat_rows, SWEEPS - sweep_index - 1
        )
    return padded


def per_device(
    perturbations, control, diffusivity, obs_cells, obs_counts, innovations, obs_precision
):
    members = lax.axis_size("mem")
    weight = 1.0 / math.sqrt(members - 1)
    member_x = perturbations[0]
    alpha_now = control[0]
    live_slots = (
        jnp.arange(obs_cells.shape[1], dtype=jnp.int32)[None, :] < obs_counts[:, None]
    ).astype(jnp.float32)
    masked_weight = obs_precision * live_slots
    kappa_rim = with_halo(diffusivity, (("lat", 1), ("lon", 2)), SWEEPS)
    for step_index in range(STEPS):
        smoothed = smooth_deep(alpha_now, kappa_rim)
        member_term = member_x.astype(jnp.float32) * smoothed
        owned_piece = lax.psum_scatter(member_term, "mem", scatter_dimension=1, tiled=True)
        increment = weight * owned_piece
        tile_cells = obs_cells[0]
        observed = increment.reshape(-1)[tile_cells]
        misfit = (observed - innovations[0]) * masked_weight[0]
        pulled = jnp.clip(misfit, -huber_edge, huber_edge) * masked_weight[0]
        tile_field = (
            jnp.zeros((increment.size,), jnp.float32)
            .at[tile_cells]
            .add(pulled)
            .reshape(increment.shape)
        )
        forcing = lax.all_gather(tile_field, "mem", axis=1, tiled=True)
        source = weight * member_x.astype(jnp.float32) * forcing
        gradient = alpha_now + adjoint_deep(source, kappa_rim)
        alpha_now = alpha_now - step_length * gradient
    return alpha_now[None]


LANES = 128
SUBLANES = 8
HALO = STEPS * SWEEPS
SLOT = 2 * HALO
GROUP = LANES // SLOT
MESH = pl.DeviceIdType.MESH


def copy_plan(members, peers, edge_tiles):
    keys = []
    for field in ("alpha", "kappa", "x"):
        keys += [(field, "row", side) for side in (-1, 1)]
    for pack in ("pack", "packx"):
        keys += [(pack, side, peer) for side in (-1, 0, 1) for peer in range(peers)]
    for step in range(STEPS):
        keys += [("sum", step, hop) for hop in range(1, members)]
        keys += [("tile", step, hop) for hop in range(1, members)]
        keys += [("edge", step, peer, hop) for peer in range(peers) for hop in range(members)]
    numbers = {key: number for number, key in enumerate(keys)}
    received = len(keys)
    for step in range(STEPS):
        for side in (-1, 1):
            numbers["row", step, side] = received
            received += edge_tiles
            for peer in range(peers):
                numbers["corner", step, side, peer] = received
                received += edge_tiles
    sent = len(keys)
    for step in range(STEPS):
        for side in (-1, 1):
            numbers["row_out", step, side] = sent
            sent += members
            for peer in range(peers):
                numbers["corner_out", step, side, peer] = sent
                sent += members
    return numbers, sent, received


def kernel(
    members,
    lat_count,
    lon_count,
    tile_rows,
    x_ref,
    control_ref,
    kappa_ref,
    cells_ref,
    counts_ref,
    innovations_ref,
    precision_ref,
    out_ref,
    x_flat,
    alpha_o,
    alpha_h,
    kappa_o,
    kappa_h,
    wx_o,
    wx_h,
    work_o,
    work_h,
    next_o,
    next_h,
    forcing_o,
    forcing_h,
    pack_out,
    pack_in,
    packx_out,
    packx_in,
    edge_out,
    edge_in,
    terms,
    pieces,
    tile_out,
    rows_hot,
    cols_hot,
    send_sems,
    recv_sems,
):
    levels = SUBLANES
    rows = control_ref.shape[0] // levels
    slots = cells_ref.shape[1]
    groups = rows // GROUP
    edge_tiles = HALO // tile_rows
    peers = [1] if lon_count == 2 else [1, lon_count - 1]
    numbers, _, _ = copy_plan(members, len(peers), edge_tiles)
    weight = 1.0 / math.sqrt(members - 1)
    mem = lax.axis_index("mem")
    lat = lax.axis_index("lat")
    lon = lax.axis_index("lon")
    has = {-1: lat > 0, 0: None, 1: lat < lat_count - 1}

    def guarded(condition, run):
        if condition is None:
            run()
        else:
            pl.when(condition)(run)

    def device(mem_hop, lat_hop, lon_hop):
        return (
            lax.rem(mem + mem_hop, members),
            lat + lat_hop,
            lax.rem(lon + lon_hop, lon_count),
        )

    def far(peer):
        return len(peers) - 1 - peer

    def remote(src, dst, send_number, recv_number, target):
        return pltpu.make_async_remote_copy(
            src_ref=src,
            dst_ref=dst,
            send_sem=send_sems.at[send_number],
            recv_sem=recv_sems.at[recv_number],
            device_id=target,
            device_id_type=MESH,
        )

    pending = []

    def send(condition, src, dst, send_number, recv_number, target):
        guarded(condition, lambda: remote(src, dst, send_number, recv_number, target).start())
        pending.append((condition, src, send_number))

    def settle(name=None):
        kept = []
        for condition, src, number in pending:
            if name is None or number in (numbers[name, "row", -1], numbers[name, "row", 1]):
                guarded(
                    condition,
                    lambda: remote(src, src, number, 0, device(0, 0, peers[0])).wait_send(),
                )
            else:
                kept.append((condition, src, number))
        pending[:] = kept

    def await_in(condition, dst, recv_number):
        guarded(
            condition,
            lambda: remote(dst, dst, 0, recv_number, device(0, 0, peers[0])).wait_recv(),
        )

    barrier = pltpu.get_barrier_semaphore()
    for lat_hop in (0, -1, 1):
        def greet(lat_hop=lat_hop):
            for lon_hop in [0] + peers:
                for mem_hop in range(members):
                    if (lat_hop, lon_hop, mem_hop) != (0, 0, 0):
                        pl.semaphore_signal(
                            barrier,
                            inc=1,
                            device_id=device(mem_hop, lat_hop, lon_hop),
                            device_id_type=MESH,
                        )
        guarded(has[lat_hop], greet)

    lane = lax.broadcasted_iota(jnp.int32, (1, SUBLANES, LANES), 2)
    lane2 = lane[0]

    x_flat[...] = weight * x_ref[...].astype(jnp.float32)
    for r in range(rows):
        level_rows = pl.ds(r, levels, stride=rows)
        alpha_o[HALO + r] = control_ref[level_rows, :]
        kappa_o[HALO + r] = kappa_ref[level_rows, :]
        wx_o[HALO + r] = x_flat[level_rows, :]

    def packed(read, count):
        total = jnp.zeros((SUBLANES, LANES), jnp.float32)
        for j in range(count):
            shifted = pltpu.roll(read(j), (HALO + SLOT * j) % LANES, 1)
            total = jnp.where(lane2 // SLOT == j, shifted, total)
        return total

    def unpacked(read, j):
        shift = (LANES - HALO - SLOT * j) % LANES
        parts = [pltpu.roll(read(peer), shift, 1) if shift else read(peer) for peer in range(len(peers))]
        if len(parts) == 1:
            return parts[0]
        return jnp.where(lane2 < LANES // 2, parts[0], parts[1])

    for g in range(groups):
        base = HALO + g * GROUP
        pack_out[g, 0] = packed(lambda j: alpha_o[base + j], GROUP)
        pack_out[g, 1] = packed(lambda j: kappa_o[base + j], GROUP)
        packx_out[g] = packed(lambda j: wx_o[base + j], GROUP)

    zero_rows = jnp.zeros((HALO, SUBLANES, LANES), jnp.float32)
    for side in (-1, 1):
        start = 0 if side < 0 else HALO + rows
        group = 0 if side < 0 else groups + 1
        tile = 0 if side < 0 else edge_tiles + members

        def clear(start=start, group=group, tile=tile):
            for ref in (alpha_o, kappa_o, wx_o, forcing_o.at[0], forcing_o.at[1]):
                ref[start : start + HALO] = zero_rows
            for peer in range(len(peers)):
                pack_in[peer, group] = jnp.zeros((2, SUBLANES, LANES), jnp.float32)
                packx_in[peer, group] = jnp.zeros((SUBLANES, LANES), jnp.float32)
                for step in range(STEPS):
                    edge_in[step, peer, tile : tile + edge_tiles] = jnp.zeros(
                        (edge_tiles, SUBLANES, LANES), jnp.float32
                    )

        guarded(jnp.logical_not(has[side]), clear)

    greeted = len(peers) + 1
    lat_near = 1 + (lat > 0).astype(jnp.int32) + (lat < lat_count - 1).astype(jnp.int32)
    pl.semaphore_wait(barrier, members * greeted * lat_near - 1)

    def row_copies(name, field, width):
        for side in (-1, 1):
            source = HALO if side < 0 else HALO + rows - width
            target = HALO + rows if side < 0 else HALO - width
            send(
                has[side],
                field.at[pl.ds(source, width)],
                field.at[pl.ds(target, width)],
                numbers[name, "row", side],
                numbers[name, "row", -side],
                device(0, side, 0),
            )

    def row_waits(name, field, width):
        for side in (-1, 1):
            start = HALO - width if side < 0 else HALO + rows
            await_in(has[side], field.at[pl.ds(start, width)], numbers[name, "row", side])

    def pack_copies(name, source, target):
        for side in (0, -1, 1):
            for peer, hop in enumerate(peers):
                if side == 0:
                    src, dst = source, target.at[far(peer), pl.ds(1, groups)]
                elif side < 0:
                    src, dst = source.at[0], target.at[far(peer), groups + 1]
                else:
                    src, dst = source.at[groups - 1], target.at[far(peer), 0]
                send(
                    has[side],
                    src,
                    dst,
                    numbers[name, side, peer],
                    numbers[name, -side, far(peer)],
                    device(0, side, hop),
                )

    def pack_waits(name, target):
        for side in (0, -1, 1):
            for peer in range(len(peers)):
                if side == 0:
                    dst = target.at[peer, pl.ds(1, groups)]
                else:
                    dst = target.at[peer, 0 if side < 0 else groups + 1]
                await_in(has[side], dst, numbers[name, side, peer])

    pack_copies("pack", pack_out, pack_in)
    row_copies("alpha", alpha_o, SWEEPS)
    row_copies("kappa", kappa_o, HALO)
    pack_copies("packx", packx_out, packx_in)
    row_copies("x", wx_o, HALO)

    cells = cells_ref[...]
    column = lax.rem(cells, LANES)
    tile_row = lax.rem(lax.div(cells, LANES), tile_rows)
    level = lax.div(cells, LANES * tile_rows)
    place = tile_row * levels + level
    spots = tile_rows * levels
    rows_hot[...] = (
        lax.broadcasted_iota(jnp.int32, (spots, slots), 0) == place
    ).astype(jnp.float32).astype(jnp.bfloat16)
    cols_hot[...] = (
        lax.broadcasted_iota(jnp.int32, (LANES, slots), 0) == column
    ).astype(jnp.float32).astype(jnp.bfloat16)
    live = (
        lax.broadcasted_iota(jnp.int32, (1, slots), 1) < counts_ref[0]
    ).astype(jnp.float32)
    masked_weight = precision_ref[...] * live
    innovations = innovations_ref[...]

    def halves(value):
        high = value.astype(jnp.bfloat16)
        return high, (value - high.astype(jnp.float32)).astype(jnp.bfloat16)

    first_lane, last_lane = lane == 0, lane == LANES - 1

    def sides(own, near):
        own_w, near_w = pltpu.roll(own, 1, 2), pltpu.roll(near, 1, 2)
        own_e, near_e = pltpu.roll(own, LANES - 1, 2), pltpu.roll(near, LANES - 1, 2)
        return (
            jnp.where(first_lane, near_w, own_w) + jnp.where(last_lane, near_e, own_e),
            jnp.where(first_lane, own_w, near_w) + jnp.where(last_lane, own_e, near_e),
        )

    def chunks(margin):
        first, last = HALO - margin, HALO + rows + margin
        return [(a, min(a + 8, last)) for a in range(first, last, 8)]

    def smooth_sweep(src, dst, margin, emit=None):
        for a, b in chunks(margin):
            own, near = src[0][a:b], src[1][a:b]
            beside = sides(own, near)
            for ref, value, both, kappa, out in (
                (src[0], own, beside[0], kappa_o, dst[0]),
                (src[1], near, beside[1], kappa_h, dst[1]),
            ):
                if emit is not None and ref is src[1]:
                    continue
                total = ref[a - 1 : b - 1] + ref[a + 1 : b + 1] + both
                value = value + kappa[a:b] * (total - 4.0 * value)
                if emit is None:
                    out[a:b] = value
                else:
                    emit(a, b, value)

    def adjoint_sweep(src, dst, margin, emit=None, near_too=True):
        for a, b in chunks(margin):
            scaled = [
                kappa[a - 1 : b + 1] * ref[a - 1 : b + 1]
                for ref, kappa in ((src[0], kappa_o), (src[1], kappa_h))
            ]
            beside = sides(scaled[0][1:-1], scaled[1][1:-1])
            for which in (0, 1):
                if which and not near_too:
                    continue
                t = scaled[which]
                value = src[which][a:b] + (t[:-2] + t[2:] + beside[which] - 4.0 * t[1:-1])
                if emit is None:
                    dst[which][a:b] = value
                else:
                    emit(which, a, b, value)

    work, following = (work_o, work_h), (next_o, next_h)

    row_waits("alpha", alpha_o, SWEEPS)
    row_waits("kappa", kappa_o, HALO)
    pack_waits("pack", pack_in)
    for e in range(rows + 2 * HALO):
        g, j = divmod(e, GROUP)
        alpha_h[e] = unpacked(lambda peer: pack_in[peer, g, 0], j)
        kappa_h[e] = unpacked(lambda peer: pack_in[peer, g, 1], j)

    for step in range(STEPS):
        term = terms.at[step]

        def emit_term(a, b, value):
            term[a - HALO : b - HALO] = wx_o[a:b] * value

        smooth_sweep((alpha_o, alpha_h), work, SWEEPS - 1)
        src, dst = work, following
        for sweep in range(1, SWEEPS):
            last = sweep == SWEEPS - 1
            smooth_sweep(src, dst, SWEEPS - 1 - sweep, emit_term if last else None)
            src, dst = dst, src

        for hop in range(1, members):
            target = lax.rem(mem + hop, members)
            send(
                None,
                term.at[pl.ds(target * tile_rows, tile_rows)],
                pieces.at[step, hop],
                numbers["sum", step, hop],
                numbers["sum", step, hop],
                device(hop, 0, 0),
            )
        total = term[pl.ds(mem * tile_rows, tile_rows)]
        if step == 0:
            row_waits("x", wx_o, HALO)
            pack_waits("packx", packx_in)
            for e in range(rows + 2 * HALO):
                g, j = divmod(e, GROUP)
                wx_h[e] = unpacked(lambda peer: packx_in[peer, g], j)
        for hop in range(1, members):
            await_in(None, pieces.at[step, hop], numbers["sum", step, hop])
            total = total + pieces[step, hop]

        flipped = jnp.transpose(total.reshape(spots, LANES))
        hot_rows, hot_cols = rows_hot[...], cols_hot[...]
        observed = jnp.zeros((LANES, slots), jnp.float32)
        for half in halves(flipped):
            observed = observed + jnp.dot(half, hot_rows, preferred_element_type=jnp.float32)
        observed = jnp.sum(
            observed * hot_cols.astype(jnp.float32), axis=0, keepdims=True
        )
        misfit = (observed - innovations) * masked_weight
        pulled = jnp.clip(misfit, -huber_edge, huber_edge) * masked_weight
        tile = jnp.zeros((spots, LANES), jnp.float32)
        for half in halves(pulled):
            tile = tile + lax.dot_general(
                hot_rows * half,
                hot_cols,
                (((1,), (1,)), ((), ())),
                preferred_element_type=jnp.float32,
            )
        tile = tile.reshape(tile_rows, SUBLANES, LANES)
        tile_out[step] = tile
        edge_out[step] = packed(lambda j: tile[j], tile_rows)

        force_o, edges = forcing_o.at[step], edge_in.at[step]
        for hop in range(1, members):
            send(
                None,
                tile_out.at[step],
                force_o.at[pl.ds(HALO + mem * tile_rows, tile_rows)],
                numbers["tile", step, hop],
                numbers["tile", step, hop],
                device(hop, 0, 0),
            )
        for side in (-1, 1):
            near = mem - (0 if side < 0 else members - edge_tiles)
            inside = near < edge_tiles if side < 0 else near >= 0
            condition = jnp.logical_and(has[side], inside)
            row = near * tile_rows + (HALO + rows if side < 0 else 0)
            spot = near + (edge_tiles + members if side < 0 else 0)
            for hop in range(members):
                send(
                    condition,
                    tile_out.at[step],
                    force_o.at[pl.ds(row, tile_rows)],
                    numbers["row_out", step, side] + hop,
                    numbers["row", step, -side] + near,
                    device(hop, side, 0),
                )
            for peer, lon_hop in enumerate(peers):
                for hop in range(members):
                    send(
                        condition,
                        edge_out.at[step],
                        edges.at[far(peer), spot],
                        numbers["corner_out", step, side, peer] + hop,
                        numbers["corner", step, -side, far(peer)] + near,
                        device(hop, side, lon_hop),
                    )
        for peer, lon_hop in enumerate(peers):
            for hop in range(members):
                send(
                    None,
                    edge_out.at[step],
                    edges.at[far(peer), edge_tiles + mem],
                    numbers["edge", step, peer, hop],
                    numbers["edge", step, far(peer), hop],
                    device(hop, 0, lon_hop),
                )
        force_o[pl.ds(HALO + mem * tile_rows, tile_rows)] = tile

        for hop in range(1, members):
            source = lax.rem(mem + members - hop, members)
            await_in(
                None,
                force_o.at[pl.ds(HALO + source * tile_rows, tile_rows)],
                numbers["tile", step, hop],
            )
        for peer in range(len(peers)):
            for hop in range(members):
                source = lax.rem(mem + members - hop, members)
                await_in(
                    None, edges.at[peer, edge_tiles + source], numbers["edge", step, peer, hop]
                )
        for side in (-1, 1):
            for i in range(edge_tiles):
                row = i * tile_rows + (0 if side < 0 else HALO + rows)
                spot = i + (0 if side < 0 else edge_tiles + members)
                await_in(
                    has[side],
                    force_o.at[pl.ds(row, tile_rows)],
                    numbers["row", step, side] + i,
                )
                for peer in range(len(peers)):
                    await_in(
                        has[side],
                        edges.at[peer, spot],
                        numbers["corner", step, side, peer] + i,
                    )

        margin = HALO - step * SWEEPS
        for e in range(HALO - margin, HALO + rows + margin):
            t, j = divmod(e, tile_rows)
            forcing_h[e] = unpacked(lambda peer: edges[peer, t], j)
        for a, b in chunks(margin):
            work_o[a:b] = wx_o[a:b] * force_o[a:b]
            work_h[a:b] = wx_h[a:b] * forcing_h[a:b]

        final = step == STEPS - 1
        inside_top = (lat > 0).astype(jnp.float32)
        inside_bottom = (lat < lat_count - 1).astype(jnp.float32)

        def emit_alpha(which, a, b, value):
            held = (alpha_o, alpha_h)[which]
            old = held[a:b]
            fresh = old - step_length * (old + value)
            if final:
                for r in range(a, b):
                    out_ref[pl.ds(r - HALO, levels, stride=rows), :] = fresh[r - a]
                return
            for r in range(a, b):
                row = fresh[r - a]
                if r < HALO:
                    row = row * inside_top
                elif r >= HALO + rows:
                    row = row * inside_bottom
                held[r] = row

        if step == 0:
            settle("alpha")
        src, dst = work, following
        for sweep in range(SWEEPS):
            last = sweep == SWEEPS - 1
            adjoint_sweep(
                src, dst, margin - 1 - sweep, emit_alpha if last else None, not (last and final)
            )
            src, dst = dst, src

    settle()


def fused(members, lat_count, lon_count, tile_rows, x, control, kappa, cells, counts, innov, prec):
    _, levels, rows, columns = x.shape
    peers = 1 if lon_count == 2 else 2
    edge_tiles = HALO // tile_rows
    slots = cells.shape[1]
    groups = rows // GROUP
    _, sent, received = copy_plan(members, peers, edge_tiles)
    vregs = lambda *lead: pltpu.VMEM(lead + (SUBLANES, LANES), jnp.float32)
    deep = rows + 2 * HALO
    tiles = members + 2 * edge_tiles
    vmem = pl.BlockSpec(memory_space=pltpu.VMEM)
    out = pl.pallas_call(
        functools.partial(kernel, members, lat_count, lon_count, tile_rows),
        out_shape=jax.ShapeDtypeStruct((levels * rows, columns), jnp.float32),
        in_specs=[vmem] * 4 + [pl.BlockSpec(memory_space=pltpu.SMEM)] + [vmem] * 2,
        out_specs=vmem,
        scratch_shapes=[pltpu.VMEM((levels * rows, columns), jnp.float32)]
        + [vregs(deep)] * 10
        + [
            vregs(STEPS, deep),
            vregs(deep),
            vregs(groups, 2),
            vregs(peers, groups + 2, 2),
            vregs(groups),
            vregs(peers, groups + 2),
            vregs(STEPS),
            vregs(STEPS, peers, tiles),
            vregs(STEPS, rows),
            vregs(STEPS, members, tile_rows),
            vregs(STEPS, tile_rows),
            pltpu.VMEM((tile_rows * levels, slots), jnp.bfloat16),
            pltpu.VMEM((LANES, slots), jnp.bfloat16),
            pltpu.SemaphoreType.DMA((sent,)),
            pltpu.SemaphoreType.DMA((received,)),
        ],
        compiler_params=pltpu.CompilerParams(collective_id=0, has_side_effects=True),
    )(
        x.reshape(levels * rows, columns),
        control.reshape(levels * rows, columns),
        kappa.reshape(levels * rows, columns),
        cells,
        counts,
        innov,
        prec,
    )
    return out.reshape(1, levels, rows, columns)


def fits(members, lat_count, lon_count, x, cells):
    _, levels, rows, columns = x.shape
    tile_rows = rows // members
    return (
        levels == SUBLANES
        and columns == LANES
        and rows % members == 0
        and rows % GROUP == 0
        and rows >= 2 * HALO
        and HALO % tile_rows == 0
        and tile_rows <= GROUP
        and HALO // tile_rows <= members
        and lon_count > 1
        and cells.shape[0] == 1
    )


def on_device(members, lat_count, lon_count, x, control, kappa, cells, counts, innov, prec):
    if not fits(members, lat_count, lon_count, x, cells):
        return per_device(x, control, kappa, cells, counts, innov, prec)
    tile_rows = x.shape[2] // members
    return fused(
        members, lat_count, lon_count, tile_rows, x, control, kappa, cells, counts, innov, prec
    )


def solution(mesh):
    return jax.shard_map(
        functools.partial(
            on_device, mesh.shape["mem"], mesh.shape["lat"], mesh.shape["lon"]
        ),
        mesh=mesh,
        in_specs=(
            P("mem", None, "lat", "lon"),
            P("mem", None, "lat", "lon"),
            P(None, "lat", "lon"),
            P(("mem", "lat", "lon"), None),
            P(("mem", "lat", "lon")),
            P(("mem", "lat", "lon"), None),
            P(("mem", "lat", "lon"), None),
        ),
        out_specs=P("mem", None, "lat", "lon"),
        check_vma=False,
    )
```

```python
import functools
import math

import jax
import jax.numpy as jnp
from jax import lax
from jax.experimental import pallas as pl
from jax.experimental.pallas import tpu as pltpu
from jax.sharding import PartitionSpec as P

SWEEPS = 4
STEPS = 2


huber_edge = 1.5
step_length = 0.5


def with_halo(cells, sides, width):
    for axis, dim in sides:
        count = lax.axis_size(axis)
        head = lax.slice_in_dim(cells, 0, width, axis=dim)
        tail = lax.slice_in_dim(cells, cells.shape[dim] - width, cells.shape[dim], axis=dim)
        cells = jnp.concatenate(
            [
                lax.ppermute(tail, axis, [(i, (i + 1) % count) for i in range(count)]),
                cells,
                lax.ppermute(head, axis, [((i + 1) % count, i) for i in range(count)]),
            ],
            axis=dim,
        )
    return cells


def inside_rows(lat_rows, margin):
    first_row = lax.axis_index("lat") * lat_rows - margin
    global_rows = first_row + jnp.arange(lat_rows + 2 * margin, dtype=jnp.int32)
    total_rows = lat_rows * lax.axis_size("lat")
    return ((global_rows >= 0) & (global_rows < total_rows)).astype(jnp.float32)[None, :, None]


def stencil(padded):
    center = padded[:, 1:-1, 1:-1]
    laplace_term = (
        padded[:, :-2, 1:-1]
        + padded[:, 2:, 1:-1]
        + padded[:, 1:-1, :-2]
        + padded[:, 1:-1, 2:]
        - 4.0 * center
    )
    return (laplace_term, center)


def smooth_deep(state_field, kappa_rim):
    lat_rows = state_field.shape[1]
    padded = with_halo(state_field, (("lat", 1), ("lon", 2)), SWEEPS)
    padded = padded * inside_rows(lat_rows, SWEEPS)
    for sweep_index in range(SWEEPS):
        offset = sweep_index + 1
        local_kappa = kappa_rim[
            :, offset : kappa_rim.shape[1] - offset, offset : kappa_rim.shape[2] - offset
        ]
        laplace_term, center = stencil(padded)
        padded = (center + local_kappa * laplace_term) * inside_rows(lat_rows, SWEEPS - offset)
    return padded


def adjoint_deep(state_field, kappa_rim):
    lat_rows = state_field.shape[1]
    padded = with_halo(state_field, (("lat", 1), ("lon", 2)), SWEEPS)
    padded = padded * inside_rows(lat_rows, SWEEPS)
    for sweep_index in range(SWEEPS):
        local_kappa = kappa_rim[
            :,
            sweep_index : kappa_rim.shape[1] - sweep_index,
            sweep_index : kappa_rim.shape[2] - sweep_index,
        ]
        laplace_term, center = stencil(local_kappa * padded)
        padded = (padded[:, 1:-1, 1:-1] + laplace_term) * inside_rows(
            lat_rows, SWEEPS - sweep_index - 1
        )
    return padded


def per_device(
    perturbations, control, diffusivity, obs_cells, obs_counts, innovations, obs_precision
):
    members = lax.axis_size("mem")
    weight = 1.0 / math.sqrt(members - 1)
    member_x = perturbations[0]
    alpha_now = control[0]
    live_slots = (
        jnp.arange(obs_cells.shape[1], dtype=jnp.int32)[None, :] < obs_counts[:, None]
    ).astype(jnp.float32)
    masked_weight = obs_precision * live_slots
    kappa_rim = with_halo(diffusivity, (("lat", 1), ("lon", 2)), SWEEPS)
    for step_index in range(STEPS):
        smoothed = smooth_deep(alpha_now, kappa_rim)
        member_term = member_x.astype(jnp.float32) * smoothed
        owned_piece = lax.psum_scatter(member_term, "mem", scatter_dimension=1, tiled=True)
        increment = weight * owned_piece
        tile_cells = obs_cells[0]
        observed = increment.reshape(-1)[tile_cells]
        misfit = (observed - innovations[0]) * masked_weight[0]
        pulled = jnp.clip(misfit, -huber_edge, huber_edge) * masked_weight[0]
        tile_field = (
            jnp.zeros((increment.size,), jnp.float32)
            .at[tile_cells]
            .add(pulled)
            .reshape(increment.shape)
        )
        forcing = lax.all_gather(tile_field, "mem", axis=1, tiled=True)
        source = weight * member_x.astype(jnp.float32) * forcing
        gradient = alpha_now + adjoint_deep(source, kappa_rim)
        alpha_now = alpha_now - step_length * gradient
    return alpha_now[None]


LANES = 128
SUBLANES = 8
HALO = STEPS * SWEEPS
SLOT = 2 * HALO
GROUP = LANES // SLOT
MESH = pl.DeviceIdType.MESH


def copy_plan(members, peers, edge_tiles):
    keys = []
    for field in ("alpha", "kappa", "kappa_far", "x"):
        keys += [(field, "row", side) for side in (-1, 1)]
    for pack in ("pack", "packx"):
        keys += [(pack, side, peer) for side in (-1, 0, 1) for peer in range(peers)]
    for step in range(STEPS):
        keys += [("sum", step, hop) for hop in range(1, members)]
        keys += [("tile", step, hop) for hop in range(1, members)]
        keys += [("edge", step, peer, hop) for peer in range(peers) for hop in range(members)]
    numbers = {key: number for number, key in enumerate(keys)}
    received = len(keys)
    for step in range(STEPS):
        for side in (-1, 1):
            numbers["row", step, side] = received
            received += edge_tiles
            for peer in range(peers):
                numbers["corner", step, side, peer] = received
                received += edge_tiles
    sent = len(keys)
    for step in range(STEPS):
        for side in (-1, 1):
            numbers["row_out", step, side] = sent
            sent += members
            for peer in range(peers):
                numbers["corner_out", step, side, peer] = sent
                sent += members
    return numbers, sent, received


def kernel(
    members,
    lat_count,
    lon_count,
    tile_rows,
    x_in,
    control_in,
    kappa_in,
    cells_in,
    counts_ref,
    innovations_in,
    precision_in,
    out_ref,
    x_ref,
    control_ref,
    kappa_ref,
    cells_ref,
    innovations_ref,
    precision_ref,
    load_sems,
    x_flat,
    alpha_o,
    alpha_h,
    kappa_o,
    kappa_h,
    wx_o,
    wx_h,
    work_o,
    work_h,
    next_o,
    next_h,
    forcing_o,
    forcing_h,
    pack_out,
    pack_in,
    packx_out,
    packx_in,
    edge_out,
    edge_in,
    terms,
    pieces,
    tile_out,
    rows_hot,
    cols_hot,
    send_sems,
    recv_sems,
):
    levels = SUBLANES
    rows = control_ref.shape[0] // levels
    slots = cells_ref.shape[1]
    groups = rows // GROUP
    edge_tiles = HALO // tile_rows
    peers = [1] if lon_count == 2 else [1, lon_count - 1]
    numbers, _, _ = copy_plan(members, len(peers), edge_tiles)
    weight = 1.0 / math.sqrt(members - 1)
    mem = lax.axis_index("mem")
    lat = lax.axis_index("lat")
    lon = lax.axis_index("lon")
    has = {-1: lat > 0, 0: None, 1: lat < lat_count - 1}

    def guarded(condition, run):
        if condition is None:
            run()
        else:
            pl.when(condition)(run)

    def device(mem_hop, lat_hop, lon_hop):
        return (
            lax.rem(mem + mem_hop, members),
            lat + lat_hop,
            lax.rem(lon + lon_hop, lon_count),
        )

    def far(peer):
        return len(peers) - 1 - peer

    def remote(src, dst, send_number, recv_number, target):
        return pltpu.make_async_remote_copy(
            src_ref=src,
            dst_ref=dst,
            send_sem=send_sems.at[send_number],
            recv_sem=recv_sems.at[recv_number],
            device_id=target,
            device_id_type=MESH,
        )

    pending = []

    def send(condition, src, dst, send_number, recv_number, target):
        guarded(condition, lambda: remote(src, dst, send_number, recv_number, target).start())
        pending.append((condition, src, send_number))

    def settle(name=None):
        kept = []
        for condition, src, number in pending:
            if name is None or number in (numbers[name, "row", -1], numbers[name, "row", 1]):
                guarded(
                    condition,
                    lambda: remote(src, src, number, 0, device(0, 0, peers[0])).wait_send(),
                )
            else:
                kept.append((condition, src, number))
        pending[:] = kept

    def await_in(condition, dst, recv_number):
        guarded(
            condition,
            lambda: remote(dst, dst, 0, recv_number, device(0, 0, peers[0])).wait_recv(),
        )

    loads = [
        pltpu.make_async_copy(src, dst, load_sems.at[number])
        for number, (src, dst) in enumerate(
            (
                (control_in, control_ref),
                (kappa_in, kappa_ref),
                (x_in, x_ref),
                (cells_in, cells_ref),
                (innovations_in, innovations_ref),
                (precision_in, precision_ref),
            )
        )
    ]
    for load in loads:
        load.start()

    barrier = pltpu.get_barrier_semaphore()
    for lat_hop in (0, -1, 1):
        def greet(lat_hop=lat_hop):
            for lon_hop in [0] + peers:
                for mem_hop in range(members):
                    if (lat_hop, lon_hop, mem_hop) != (0, 0, 0):
                        pl.semaphore_signal(
                            barrier,
                            inc=1,
                            device_id=device(mem_hop, lat_hop, lon_hop),
                            device_id_type=MESH,
                        )
        guarded(has[lat_hop], greet)

    lane = lax.broadcasted_iota(jnp.int32, (1, SUBLANES, LANES), 2)
    lane2 = lane[0]

    for load in loads:
        load.wait()
    x_flat[...] = weight * x_ref[...].astype(jnp.float32)
    for r in range(rows):
        level_rows = pl.ds(r, levels, stride=rows)
        alpha_o[HALO + r] = control_ref[level_rows, :]
        kappa_o[HALO + r] = kappa_ref[level_rows, :]
        wx_o[HALO + r] = x_flat[level_rows, :]

    def packed(read, count):
        total = jnp.zeros((SUBLANES, LANES), jnp.float32)
        for j in range(count):
            shifted = pltpu.roll(read(j), (HALO + SLOT * j) % LANES, 1)
            total = jnp.where(lane2 // SLOT == j, shifted, total)
        return total

    def unpacked(read, j):
        shift = (LANES - HALO - SLOT * j) % LANES
        parts = [pltpu.roll(read(peer), shift, 1) if shift else read(peer) for peer in range(len(peers))]
        if len(parts) == 1:
            return parts[0]
        return jnp.where(lane2 < LANES // 2, parts[0], parts[1])

    for g in range(groups):
        base = HALO + g * GROUP
        pack_out[g, 0] = packed(lambda j: alpha_o[base + j], GROUP)
        pack_out[g, 1] = packed(lambda j: kappa_o[base + j], GROUP)
        packx_out[g] = packed(lambda j: wx_o[base + j], GROUP)

    zero_rows = jnp.zeros((HALO, SUBLANES, LANES), jnp.float32)
    for side in (-1, 1):
        start = 0 if side < 0 else HALO + rows
        group = 0 if side < 0 else groups + 1
        tile = 0 if side < 0 else edge_tiles + members

        def clear(start=start, group=group, tile=tile):
            for ref in (alpha_o, kappa_o, wx_o, forcing_o.at[0], forcing_o.at[1]):
                ref[start : start + HALO] = zero_rows
            for peer in range(len(peers)):
                pack_in[peer, group] = jnp.zeros((2, SUBLANES, LANES), jnp.float32)
                packx_in[peer, group] = jnp.zeros((SUBLANES, LANES), jnp.float32)
                for step in range(STEPS):
                    edge_in[step, peer, tile : tile + edge_tiles] = jnp.zeros(
                        (edge_tiles, SUBLANES, LANES), jnp.float32
                    )

        guarded(jnp.logical_not(has[side]), clear)

    greeted = len(peers) + 1
    lat_near = 1 + (lat > 0).astype(jnp.int32) + (lat < lat_count - 1).astype(jnp.int32)
    pl.semaphore_wait(barrier, members * greeted * lat_near - 1)

    def row_copies(name, field, width, skip=0):
        for side in (-1, 1):
            source = HALO + skip if side < 0 else HALO + rows - width - skip
            target = HALO + rows + skip if side < 0 else HALO - width - skip
            send(
                has[side],
                field.at[pl.ds(source, width)],
                field.at[pl.ds(target, width)],
                numbers[name, "row", side],
                numbers[name, "row", -side],
                device(0, side, 0),
            )

    def row_waits(name, field, width, skip=0):
        for side in (-1, 1):
            start = HALO - width - skip if side < 0 else HALO + rows + skip
            await_in(has[side], field.at[pl.ds(start, width)], numbers[name, "row", side])

    def pack_copies(name, source, target):
        for side in (0, -1, 1):
            for peer, hop in enumerate(peers):
                if side == 0:
                    src, dst = source, target.at[far(peer), pl.ds(1, groups)]
                elif side < 0:
                    src, dst = source.at[0], target.at[far(peer), groups + 1]
                else:
                    src, dst = source.at[groups - 1], target.at[far(peer), 0]
                send(
                    has[side],
                    src,
                    dst,
                    numbers[name, side, peer],
                    numbers[name, -side, far(peer)],
                    device(0, side, hop),
                )

    def pack_waits(name, target):
        for side in (0, -1, 1):
            for peer in range(len(peers)):
                if side == 0:
                    dst = target.at[peer, pl.ds(1, groups)]
                else:
                    dst = target.at[peer, 0 if side < 0 else groups + 1]
                await_in(has[side], dst, numbers[name, side, peer])

    pack_copies("pack", pack_out, pack_in)
    row_copies("alpha", alpha_o, SWEEPS)
    row_copies("kappa", kappa_o, SWEEPS)
    pack_copies("packx", packx_out, packx_in)
    row_copies("kappa_far", kappa_o, HALO - SWEEPS, SWEEPS)
    row_copies("x", wx_o, HALO)

    cells = cells_ref[...]
    column = lax.rem(cells, LANES)
    tile_row = lax.rem(lax.div(cells, LANES), tile_rows)
    level = lax.div(cells, LANES * tile_rows)
    place = tile_row * levels + level
    spots = tile_rows * levels
    rows_hot[...] = (
        lax.broadcasted_iota(jnp.int32, (spots, slots), 0) == place
    ).astype(jnp.float32).astype(jnp.bfloat16)
    cols_hot[...] = (
        lax.broadcasted_iota(jnp.int32, (LANES, slots), 0) == column
    ).astype(jnp.float32).astype(jnp.bfloat16)
    live = (
        lax.broadcasted_iota(jnp.int32, (1, slots), 1) < counts_ref[0]
    ).astype(jnp.float32)
    masked_weight = precision_ref[...] * live
    innovations = innovations_ref[...]

    def halves(value):
        high = value.astype(jnp.bfloat16)
        return high, (value - high.astype(jnp.float32)).astype(jnp.bfloat16)

    first_lane, last_lane = lane == 0, lane == LANES - 1

    def sides(own, near):
        own_w, near_w = pltpu.roll(own, 1, 2), pltpu.roll(near, 1, 2)
        own_e, near_e = pltpu.roll(own, LANES - 1, 2), pltpu.roll(near, LANES - 1, 2)
        return (
            jnp.where(first_lane, near_w, own_w) + jnp.where(last_lane, near_e, own_e),
            jnp.where(first_lane, own_w, near_w) + jnp.where(last_lane, own_e, near_e),
        )

    def chunks(margin):
        first, last = HALO - margin, HALO + rows + margin
        return [(a, min(a + 8, last)) for a in range(first, last, 8)]

    def smooth_sweep(src, dst, margin, emit=None):
        for a, b in chunks(margin):
            own, near = src[0][a:b], src[1][a:b]
            beside = sides(own, near)
            for ref, value, both, kappa, out in (
                (src[0], own, beside[0], kappa_o, dst[0]),
                (src[1], near, beside[1], kappa_h, dst[1]),
            ):
                if emit is not None and ref is src[1]:
                    continue
                total = ref[a - 1 : b - 1] + ref[a + 1 : b + 1] + both
                value = value + kappa[a:b] * (total - 4.0 * value)
                if emit is None:
                    out[a:b] = value
                else:
                    emit(a, b, value)

    def adjoint_sweep(src, dst, margin, emit=None, near_too=True):
        for a, b in chunks(margin):
            scaled = [
                kappa[a - 1 : b + 1] * ref[a - 1 : b + 1]
                for ref, kappa in ((src[0], kappa_o), (src[1], kappa_h))
            ]
            beside = sides(scaled[0][1:-1], scaled[1][1:-1])
            for which in (0, 1):
                if which and not near_too:
                    continue
                t = scaled[which]
                value = src[which][a:b] + (t[:-2] + t[2:] + beside[which] - 4.0 * t[1:-1])
                if emit is None:
                    dst[which][a:b] = value
                else:
                    emit(which, a, b, value)

    work, following = (work_o, work_h), (next_o, next_h)

    row_waits("alpha", alpha_o, SWEEPS)
    row_waits("kappa", kappa_o, SWEEPS)
    pack_waits("pack", pack_in)
    for e in range(rows + 2 * HALO):
        g, j = divmod(e, GROUP)
        alpha_h[e] = unpacked(lambda peer: pack_in[peer, g, 0], j)
        kappa_h[e] = unpacked(lambda peer: pack_in[peer, g, 1], j)

    for step in range(STEPS):
        term = terms.at[step]

        def emit_term(a, b, value):
            term[a - HALO : b - HALO] = wx_o[a:b] * value

        smooth_sweep((alpha_o, alpha_h), work, SWEEPS - 1)
        src, dst = work, following
        for sweep in range(1, SWEEPS):
            last = sweep == SWEEPS - 1
            smooth_sweep(src, dst, SWEEPS - 1 - sweep, emit_term if last else None)
            src, dst = dst, src

        for hop in range(1, members):
            target = lax.rem(mem + hop, members)
            send(
                None,
                term.at[pl.ds(target * tile_rows, tile_rows)],
                pieces.at[step, hop],
                numbers["sum", step, hop],
                numbers["sum", step, hop],
                device(hop, 0, 0),
            )
        total = term[pl.ds(mem * tile_rows, tile_rows)]
        if step == 0:
            row_waits("kappa_far", kappa_o, HALO - SWEEPS, SWEEPS)
            row_waits("x", wx_o, HALO)
            pack_waits("packx", packx_in)
            for e in range(rows + 2 * HALO):
                g, j = divmod(e, GROUP)
                wx_h[e] = unpacked(lambda peer: packx_in[peer, g], j)
        for hop in range(1, members):
            await_in(None, pieces.at[step, hop], numbers["sum", step, hop])
            total = total + pieces[step, hop]

        flipped = jnp.transpose(total.reshape(spots, LANES))
        hot_rows, hot_cols = rows_hot[...], cols_hot[...]
        observed = jnp.zeros((LANES, slots), jnp.float32)
        for half in halves(flipped):
            observed = observed + jnp.dot(half, hot_rows, preferred_element_type=jnp.float32)
        observed = jnp.sum(
            observed * hot_cols.astype(jnp.float32), axis=0, keepdims=True
        )
        misfit = (observed - innovations) * masked_weight
        pulled = jnp.clip(misfit, -huber_edge, huber_edge) * masked_weight
        tile = jnp.zeros((spots, LANES), jnp.float32)
        for half in halves(pulled):
            tile = tile + lax.dot_general(
                hot_rows * half,
                hot_cols,
                (((1,), (1,)), ((), ())),
                preferred_element_type=jnp.float32,
            )
        tile = tile.reshape(tile_rows, SUBLANES, LANES)
        tile_out[step] = tile
        edge_out[step] = packed(lambda j: tile[j], tile_rows)

        force_o, edges = forcing_o.at[step], edge_in.at[step]
        for hop in range(1, members):
            send(
                None,
                tile_out.at[step],
                force_o.at[pl.ds(HALO + mem * tile_rows, tile_rows)],
                numbers["tile", step, hop],
                numbers["tile", step, hop],
                device(hop, 0, 0),
            )
        for side in (-1, 1):
            near = mem - (0 if side < 0 else members - edge_tiles)
            inside = near < edge_tiles if side < 0 else near >= 0
            condition = jnp.logical_and(has[side], inside)
            row = near * tile_rows + (HALO + rows if side < 0 else 0)
            spot = near + (edge_tiles + members if side < 0 else 0)
            for hop in range(members):
                send(
                    condition,
                    tile_out.at[step],
                    force_o.at[pl.ds(row, tile_rows)],
                    numbers["row_out", step, side] + hop,
                    numbers["row", step, -side] + near,
                    device(hop, side, 0),
                )
            for peer, lon_hop in enumerate(peers):
                for hop in range(members):
                    send(
                        condition,
                        edge_out.at[step],
                        edges.at[far(peer), spot],
                        numbers["corner_out", step, side, peer] + hop,
                        numbers["corner", step, -side, far(peer)] + near,
                        device(hop, side, lon_hop),
                    )
        for peer, lon_hop in enumerate(peers):
            for hop in range(members):
                send(
                    None,
                    edge_out.at[step],
                    edges.at[far(peer), edge_tiles + mem],
                    numbers["edge", step, peer, hop],
                    numbers["edge", step, far(peer), hop],
                    device(hop, 0, lon_hop),
                )
        force_o[pl.ds(HALO + mem * tile_rows, tile_rows)] = tile

        for hop in range(1, members):
            source = lax.rem(mem + members - hop, members)
            await_in(
                None,
                force_o.at[pl.ds(HALO + source * tile_rows, tile_rows)],
                numbers["tile", step, hop],
            )
        for peer in range(len(peers)):
            for hop in range(members):
                source = lax.rem(mem + members - hop, members)
                await_in(
                    None, edges.at[peer, edge_tiles + source], numbers["edge", step, peer, hop]
                )
        for side in (-1, 1):
            for i in range(edge_tiles):
                row = i * tile_rows + (0 if side < 0 else HALO + rows)
                spot = i + (0 if side < 0 else edge_tiles + members)
                await_in(
                    has[side],
                    force_o.at[pl.ds(row, tile_rows)],
                    numbers["row", step, side] + i,
                )
                for peer in range(len(peers)):
                    await_in(
                        has[side],
                        edges.at[peer, spot],
                        numbers["corner", step, side, peer] + i,
                    )

        margin = HALO - step * SWEEPS
        for e in range(HALO - margin, HALO + rows + margin):
            t, j = divmod(e, tile_rows)
            forcing_h[e] = unpacked(lambda peer: edges[peer, t], j)
        for a, b in chunks(margin):
            work_o[a:b] = wx_o[a:b] * force_o[a:b]
            work_h[a:b] = wx_h[a:b] * forcing_h[a:b]

        final = step == STEPS - 1
        inside_top = (lat > 0).astype(jnp.float32)
        inside_bottom = (lat < lat_count - 1).astype(jnp.float32)

        def emit_alpha(which, a, b, value):
            held = (alpha_o, alpha_h)[which]
            old = held[a:b]
            if final:
                fresh = ((1.0 - step_length) / step_length) * old - value
                for r in range(a, b):
                    out_ref[pl.ds(r - HALO, levels, stride=rows), :] = fresh[r - a]
                return
            fresh = old - step_length * (old + value)
            for r in range(a, b):
                row = fresh[r - a]
                if r < HALO:
                    row = row * inside_top
                elif r >= HALO + rows:
                    row = row * inside_bottom
                held[r] = row

        if step == 0:
            settle("alpha")
        src, dst = work, following
        for sweep in range(SWEEPS):
            last = sweep == SWEEPS - 1
            adjoint_sweep(
                src, dst, margin - 1 - sweep, emit_alpha if last else None, not (last and final)
            )
            src, dst = dst, src

    settle()


def fused(members, lat_count, lon_count, tile_rows, x, control, kappa, cells, counts, innov, prec):
    _, levels, rows, columns = x.shape
    peers = 1 if lon_count == 2 else 2
    edge_tiles = HALO // tile_rows
    slots = cells.shape[1]
    groups = rows // GROUP
    _, sent, received = copy_plan(members, peers, edge_tiles)
    vregs = lambda *lead: pltpu.VMEM(lead + (SUBLANES, LANES), jnp.float32)
    deep = rows + 2 * HALO
    tiles = members + 2 * edge_tiles
    vmem = pl.BlockSpec(memory_space=pltpu.VMEM)
    place = pl.BlockSpec(memory_space=pl.ANY)
    flat = lambda dtype: pltpu.VMEM((levels * rows, columns), dtype)
    out = pl.pallas_call(
        functools.partial(kernel, members, lat_count, lon_count, tile_rows),
        out_shape=jax.ShapeDtypeStruct((levels * rows, columns), jnp.float32),
        in_specs=[place] * 4 + [pl.BlockSpec(memory_space=pltpu.SMEM)] + [place] * 2,
        out_specs=vmem,
        scratch_shapes=[
            flat(x.dtype),
            flat(jnp.float32),
            flat(jnp.float32),
            pltpu.VMEM(cells.shape, cells.dtype),
            pltpu.VMEM(innov.shape, innov.dtype),
            pltpu.VMEM(prec.shape, prec.dtype),
            pltpu.SemaphoreType.DMA((6,)),
            flat(jnp.float32),
        ]
        + [vregs(deep)] * 10
        + [
            vregs(STEPS, deep),
            vregs(deep),
            vregs(groups, 2),
            vregs(peers, groups + 2, 2),
            vregs(groups),
            vregs(peers, groups + 2),
            vregs(STEPS),
            vregs(STEPS, peers, tiles),
            vregs(STEPS, rows),
            vregs(STEPS, members, tile_rows),
            vregs(STEPS, tile_rows),
            pltpu.VMEM((tile_rows * levels, slots), jnp.bfloat16),
            pltpu.VMEM((LANES, slots), jnp.bfloat16),
            pltpu.SemaphoreType.DMA((sent,)),
            pltpu.SemaphoreType.DMA((received,)),
        ],
        compiler_params=pltpu.CompilerParams(collective_id=0, has_side_effects=True),
    )(
        x.reshape(levels * rows, columns),
        control.reshape(levels * rows, columns),
        kappa.reshape(levels * rows, columns),
        cells,
        counts,
        innov,
        prec,
    )
    return (step_length * out).reshape(1, levels, rows, columns)


def fits(members, lat_count, lon_count, x, cells):
    _, levels, rows, columns = x.shape
    tile_rows = rows // members
    return (
        levels == SUBLANES
        and columns == LANES
        and rows % members == 0
        and rows % GROUP == 0
        and rows >= 2 * HALO
        and HALO % tile_rows == 0
        and tile_rows <= GROUP
        and HALO // tile_rows <= members
        and lon_count > 1
        and cells.shape[0] == 1
    )


def on_device(members, lat_count, lon_count, x, control, kappa, cells, counts, innov, prec):
    if not fits(members, lat_count, lon_count, x, cells):
        return per_device(x, control, kappa, cells, counts, innov, prec)
    tile_rows = x.shape[2] // members
    return fused(
        members, lat_count, lon_count, tile_rows, x, control, kappa, cells, counts, innov, prec
    )


def solution(mesh):
    return jax.shard_map(
        functools.partial(
            on_device, mesh.shape["mem"], mesh.shape["lat"], mesh.shape["lon"]
        ),
        mesh=mesh,
        in_specs=(
            P("mem", None, "lat", "lon"),
            P("mem", None, "lat", "lon"),
            P(None, "lat", "lon"),
            P(("mem", "lat", "lon"), None),
            P(("mem", "lat", "lon")),
            P(("mem", "lat", "lon"), None),
            P(("mem", "lat", "lon"), None),
        ),
        out_specs=P("mem", None, "lat", "lon"),
        check_vma=False,
    )
```

```python
import functools
import math

import jax
import jax.numpy as jnp
from jax import lax
from jax.experimental import pallas as pl
from jax.experimental.pallas import tpu as pltpu
from jax.sharding import PartitionSpec as P

SWEEPS = 4
STEPS = 2


huber_edge = 1.5
step_length = 0.5


def with_halo(cells, sides, width):
    for axis, dim in sides:
        count = lax.axis_size(axis)
        head = lax.slice_in_dim(cells, 0, width, axis=dim)
        tail = lax.slice_in_dim(cells, cells.shape[dim] - width, cells.shape[dim], axis=dim)
        cells = jnp.concatenate(
            [
                lax.ppermute(tail, axis, [(i, (i + 1) % count) for i in range(count)]),
                cells,
                lax.ppermute(head, axis, [((i + 1) % count, i) for i in range(count)]),
            ],
            axis=dim,
        )
    return cells


def inside_rows(lat_rows, margin):
    first_row = lax.axis_index("lat") * lat_rows - margin
    global_rows = first_row + jnp.arange(lat_rows + 2 * margin, dtype=jnp.int32)
    total_rows = lat_rows * lax.axis_size("lat")
    return ((global_rows >= 0) & (global_rows < total_rows)).astype(jnp.float32)[None, :, None]


def stencil(padded):
    center = padded[:, 1:-1, 1:-1]
    laplace_term = (
        padded[:, :-2, 1:-1]
        + padded[:, 2:, 1:-1]
        + padded[:, 1:-1, :-2]
        + padded[:, 1:-1, 2:]
        - 4.0 * center
    )
    return (laplace_term, center)


def smooth_deep(state_field, kappa_rim):
    lat_rows = state_field.shape[1]
    padded = with_halo(state_field, (("lat", 1), ("lon", 2)), SWEEPS)
    padded = padded * inside_rows(lat_rows, SWEEPS)
    for sweep_index in range(SWEEPS):
        offset = sweep_index + 1
        local_kappa = kappa_rim[
            :, offset : kappa_rim.shape[1] - offset, offset : kappa_rim.shape[2] - offset
        ]
        laplace_term, center = stencil(padded)
        padded = (center + local_kappa * laplace_term) * inside_rows(lat_rows, SWEEPS - offset)
    return padded


def adjoint_deep(state_field, kappa_rim):
    lat_rows = state_field.shape[1]
    padded = with_halo(state_field, (("lat", 1), ("lon", 2)), SWEEPS)
    padded = padded * inside_rows(lat_rows, SWEEPS)
    for sweep_index in range(SWEEPS):
        local_kappa = kappa_rim[
            :,
            sweep_index : kappa_rim.shape[1] - sweep_index,
            sweep_index : kappa_rim.shape[2] - sweep_index,
        ]
        laplace_term, center = stencil(local_kappa * padded)
        padded = (padded[:, 1:-1, 1:-1] + laplace_term) * inside_rows(
            lat_rows, SWEEPS - sweep_index - 1
        )
    return padded


def per_device(
    perturbations, control, diffusivity, obs_cells, obs_counts, innovations, obs_precision
):
    members = lax.axis_size("mem")
    weight = 1.0 / math.sqrt(members - 1)
    member_x = perturbations[0]
    alpha_now = control[0]
    live_slots = (
        jnp.arange(obs_cells.shape[1], dtype=jnp.int32)[None, :] < obs_counts[:, None]
    ).astype(jnp.float32)
    masked_weight = obs_precision * live_slots
    kappa_rim = with_halo(diffusivity, (("lat", 1), ("lon", 2)), SWEEPS)
    for step_index in range(STEPS):
        smoothed = smooth_deep(alpha_now, kappa_rim)
        member_term = member_x.astype(jnp.float32) * smoothed
        owned_piece = lax.psum_scatter(member_term, "mem", scatter_dimension=1, tiled=True)
        increment = weight * owned_piece
        tile_cells = obs_cells[0]
        observed = increment.reshape(-1)[tile_cells]
        misfit = (observed - innovations[0]) * masked_weight[0]
        pulled = jnp.clip(misfit, -huber_edge, huber_edge) * masked_weight[0]
        tile_field = (
            jnp.zeros((increment.size,), jnp.float32)
            .at[tile_cells]
            .add(pulled)
            .reshape(increment.shape)
        )
        forcing = lax.all_gather(tile_field, "mem", axis=1, tiled=True)
        source = weight * member_x.astype(jnp.float32) * forcing
        gradient = alpha_now + adjoint_deep(source, kappa_rim)
        alpha_now = alpha_now - step_length * gradient
    return alpha_now[None]


LANES = 128
SUBLANES = 8
HALO = STEPS * SWEEPS
SLOT = 2 * HALO
GROUP = LANES // SLOT
MESH = pl.DeviceIdType.MESH


def copy_plan(members, peers, edge_tiles):
    keys = []
    for field in ("alpha", "kappa", "kappa_far", "x"):
        keys += [(field, "row", side) for side in (-1, 1)]
    for pack in ("pack", "packx"):
        keys += [(pack, side, peer) for side in (-1, 0, 1) for peer in range(peers)]
    keys += [("cells", hop) for hop in range(1, members)]
    for step in range(STEPS):
        keys += [("sum", step, hop) for hop in range(1, members)]
        keys += [("tile", step, hop) for hop in range(1, members)]
        keys += [("edge", step, peer, hop) for peer in range(peers) for hop in range(members)]
    numbers = {key: number for number, key in enumerate(keys)}
    received = len(keys)
    for side in (-1, 1):
        numbers["cells_row", side] = received
        received += edge_tiles
    for step in range(STEPS):
        for side in (-1, 1):
            numbers["row", step, side] = received
            received += edge_tiles
            for peer in range(peers):
                numbers["corner", step, side, peer] = received
                received += edge_tiles
    sent = len(keys)
    for side in (-1, 1):
        numbers["cells_out", side] = sent
        sent += members
    for step in range(STEPS):
        for side in (-1, 1):
            numbers["row_out", step, side] = sent
            sent += members
            for peer in range(peers):
                numbers["corner_out", step, side, peer] = sent
                sent += members
    return numbers, sent, received


def kernel(
    members,
    lat_count,
    lon_count,
    tile_rows,
    x_in,
    control_in,
    kappa_in,
    cells_in,
    counts_ref,
    innovations_in,
    precision_in,
    out_ref,
    x_ref,
    control_ref,
    kappa_ref,
    cells_ref,
    innovations_ref,
    precision_ref,
    load_sems,
    x_flat,
    alpha_o,
    alpha_h,
    kappa_o,
    kappa_h,
    wx_o,
    wx_h,
    work_o,
    work_h,
    next_o,
    next_h,
    forcing_o,
    forcing_h,
    pack_out,
    pack_in,
    packx_out,
    packx_in,
    edge_out,
    edge_in,
    terms,
    pieces,
    pulled_out,
    pulled_in,
    cells_all,
    rows_hot,
    cols_hot,
    send_sems,
    recv_sems,
):
    levels = SUBLANES
    rows = control_ref.shape[0] // levels
    slots = cells_ref.shape[1]
    groups = rows // GROUP
    edge_tiles = HALO // tile_rows
    peers = [1] if lon_count == 2 else [1, lon_count - 1]
    numbers, _, _ = copy_plan(members, len(peers), edge_tiles)
    weight = 1.0 / math.sqrt(members - 1)
    mem = lax.axis_index("mem")
    lat = lax.axis_index("lat")
    lon = lax.axis_index("lon")
    has = {-1: lat > 0, 0: None, 1: lat < lat_count - 1}

    def guarded(condition, run):
        if condition is None:
            run()
        else:
            pl.when(condition)(run)

    def device(mem_hop, lat_hop, lon_hop):
        return (
            lax.rem(mem + mem_hop, members),
            lat + lat_hop,
            lax.rem(lon + lon_hop, lon_count),
        )

    def far(peer):
        return len(peers) - 1 - peer

    def remote(src, dst, send_number, recv_number, target):
        return pltpu.make_async_remote_copy(
            src_ref=src,
            dst_ref=dst,
            send_sem=send_sems.at[send_number],
            recv_sem=recv_sems.at[recv_number],
            device_id=target,
            device_id_type=MESH,
        )

    pending = []

    def send(condition, src, dst, send_number, recv_number, target):
        guarded(condition, lambda: remote(src, dst, send_number, recv_number, target).start())
        pending.append((condition, src, send_number))

    def settle(name=None):
        kept = []
        for condition, src, number in pending:
            if name is None or number in (numbers[name, "row", -1], numbers[name, "row", 1]):
                guarded(
                    condition,
                    lambda: remote(src, src, number, 0, device(0, 0, peers[0])).wait_send(),
                )
            else:
                kept.append((condition, src, number))
        pending[:] = kept

    def await_in(condition, dst, recv_number):
        guarded(
            condition,
            lambda: remote(dst, dst, 0, recv_number, device(0, 0, peers[0])).wait_recv(),
        )

    loads = [
        pltpu.make_async_copy(src, dst, load_sems.at[number])
        for number, (src, dst) in enumerate(
            (
                (control_in, control_ref),
                (kappa_in, kappa_ref),
                (x_in, x_ref),
                (cells_in, cells_ref),
                (innovations_in, innovations_ref),
                (precision_in, precision_ref),
            )
        )
    ]
    for load in loads:
        load.start()

    barrier = pltpu.get_barrier_semaphore()
    for lat_hop in (0, -1, 1):
        def greet(lat_hop=lat_hop):
            for lon_hop in [0] + peers:
                for mem_hop in range(members):
                    if (lat_hop, lon_hop, mem_hop) != (0, 0, 0):
                        pl.semaphore_signal(
                            barrier,
                            inc=1,
                            device_id=device(mem_hop, lat_hop, lon_hop),
                            device_id_type=MESH,
                        )
        guarded(has[lat_hop], greet)

    lane = lax.broadcasted_iota(jnp.int32, (1, SUBLANES, LANES), 2)
    lane2 = lane[0]

    for load in loads:
        load.wait()
    x_flat[...] = weight * x_ref[...].astype(jnp.float32)
    for r in range(rows):
        level_rows = pl.ds(r, levels, stride=rows)
        alpha_o[HALO + r] = control_ref[level_rows, :]
        kappa_o[HALO + r] = kappa_ref[level_rows, :]
        wx_o[HALO + r] = x_flat[level_rows, :]

    def packed(read, count):
        total = jnp.zeros((SUBLANES, LANES), jnp.float32)
        for j in range(count):
            shifted = pltpu.roll(read(j), (HALO + SLOT * j) % LANES, 1)
            total = jnp.where(lane2 // SLOT == j, shifted, total)
        return total

    def unpacked(read, j):
        shift = (LANES - HALO - SLOT * j) % LANES
        parts = [pltpu.roll(read(peer), shift, 1) if shift else read(peer) for peer in range(len(peers))]
        if len(parts) == 1:
            return parts[0]
        return jnp.where(lane2 < LANES // 2, parts[0], parts[1])

    for g in range(groups):
        base = HALO + g * GROUP
        pack_out[g, 0] = packed(lambda j: alpha_o[base + j], GROUP)
        pack_out[g, 1] = packed(lambda j: kappa_o[base + j], GROUP)
        packx_out[g] = packed(lambda j: wx_o[base + j], GROUP)

    zero_rows = jnp.zeros((HALO, SUBLANES, LANES), jnp.float32)
    for side in (-1, 1):
        start = 0 if side < 0 else HALO + rows
        group = 0 if side < 0 else groups + 1
        tile = 0 if side < 0 else edge_tiles + members

        def clear(start=start, group=group, tile=tile):
            for ref in (alpha_o, kappa_o, wx_o):
                ref[start : start + HALO] = zero_rows
            cells_all[tile : tile + edge_tiles] = jnp.zeros((edge_tiles, 1, slots), jnp.int32)
            for step in range(STEPS):
                pulled_in[step, tile : tile + edge_tiles] = jnp.zeros(
                    (edge_tiles, 1, slots), jnp.float32
                )
            for peer in range(len(peers)):
                pack_in[peer, group] = jnp.zeros((2, SUBLANES, LANES), jnp.float32)
                packx_in[peer, group] = jnp.zeros((SUBLANES, LANES), jnp.float32)
                for step in range(STEPS):
                    edge_in[step, peer, tile : tile + edge_tiles] = jnp.zeros(
                        (edge_tiles, SUBLANES, LANES), jnp.float32
                    )

        guarded(jnp.logical_not(has[side]), clear)

    greeted = len(peers) + 1
    lat_near = 1 + (lat > 0).astype(jnp.int32) + (lat < lat_count - 1).astype(jnp.int32)
    pl.semaphore_wait(barrier, members * greeted * lat_near - 1)

    def row_copies(name, field, width, skip=0):
        for side in (-1, 1):
            source = HALO + skip if side < 0 else HALO + rows - width - skip
            target = HALO + rows + skip if side < 0 else HALO - width - skip
            send(
                has[side],
                field.at[pl.ds(source, width)],
                field.at[pl.ds(target, width)],
                numbers[name, "row", side],
                numbers[name, "row", -side],
                device(0, side, 0),
            )

    def row_waits(name, field, width, skip=0):
        for side in (-1, 1):
            start = HALO - width - skip if side < 0 else HALO + rows + skip
            await_in(has[side], field.at[pl.ds(start, width)], numbers[name, "row", side])

    def pack_copies(name, source, target):
        for side in (0, -1, 1):
            for peer, hop in enumerate(peers):
                if side == 0:
                    src, dst = source, target.at[far(peer), pl.ds(1, groups)]
                elif side < 0:
                    src, dst = source.at[0], target.at[far(peer), groups + 1]
                else:
                    src, dst = source.at[groups - 1], target.at[far(peer), 0]
                send(
                    has[side],
                    src,
                    dst,
                    numbers[name, side, peer],
                    numbers[name, -side, far(peer)],
                    device(0, side, hop),
                )

    def pack_waits(name, target):
        for side in (0, -1, 1):
            for peer in range(len(peers)):
                if side == 0:
                    dst = target.at[peer, pl.ds(1, groups)]
                else:
                    dst = target.at[peer, 0 if side < 0 else groups + 1]
                await_in(has[side], dst, numbers[name, side, peer])

    pack_copies("pack", pack_out, pack_in)
    row_copies("alpha", alpha_o, SWEEPS)
    row_copies("kappa", kappa_o, SWEEPS)
    pack_copies("packx", packx_out, packx_in)
    row_copies("kappa_far", kappa_o, HALO - SWEEPS, SWEEPS)
    row_copies("x", wx_o, HALO)

    def to_group(step, source, target, name):
        for hop in range(1, members):
            send(
                None,
                source,
                target.at[edge_tiles + mem],
                numbers[name + (hop,)],
                numbers[name + (hop,)],
                device(hop, 0, 0),
            )
        outs, ins = ("cells_out", "cells_row") if step is None else ("row_out", "row")
        key = () if step is None else (step,)
        for side in (-1, 1):
            near = mem - (0 if side < 0 else members - edge_tiles)
            inside = near < edge_tiles if side < 0 else near >= 0
            for hop in range(members):
                send(
                    jnp.logical_and(has[side], inside),
                    source,
                    target.at[near + (edge_tiles + members if side < 0 else 0)],
                    numbers[(outs,) + key + (side,)] + hop,
                    numbers[(ins,) + key + (-side,)] + near,
                    device(hop, side, 0),
                )

    def others():
        for hop in range(1, members):
            yield None, hop, edge_tiles + lax.rem(mem + members - hop, members)
        for side in (-1, 1):
            for i in range(edge_tiles):
                yield side, i, i + (0 if side < 0 else edge_tiles + members)

    to_group(None, cells_ref, cells_all, ("cells",))

    spots = tile_rows * levels

    def hot(spot, cells):
        column = lax.rem(cells, LANES)
        tile_row = lax.rem(lax.div(cells, LANES), tile_rows)
        level = lax.div(cells, LANES * tile_rows)
        place = tile_row * levels + level
        rows_hot[spot] = (
            lax.broadcasted_iota(jnp.int32, (spots, slots), 0) == place
        ).astype(jnp.float32).astype(jnp.bfloat16)
        cols_hot[spot] = (
            lax.broadcasted_iota(jnp.int32, (LANES, slots), 0) == column
        ).astype(jnp.float32).astype(jnp.bfloat16)

    def spread(spot, pulled):
        tile = jnp.zeros((spots, LANES), jnp.float32)
        for half in halves(pulled):
            tile = tile + lax.dot_general(
                rows_hot[spot] * half,
                cols_hot[spot],
                (((1,), (1,)), ((), ())),
                preferred_element_type=jnp.float32,
            )
        return tile.reshape(tile_rows, SUBLANES, LANES)

    mine = edge_tiles + mem
    hot(mine, cells_ref[...])
    live = (
        lax.broadcasted_iota(jnp.int32, (1, slots), 1) < counts_ref[0]
    ).astype(jnp.float32)
    masked_weight = precision_ref[...] * live
    innovations = innovations_ref[...]

    def halves(value):
        high = value.astype(jnp.bfloat16)
        return high, (value - high.astype(jnp.float32)).astype(jnp.bfloat16)

    first_lane, last_lane = lane == 0, lane == LANES - 1

    def sides(own, near):
        own_w, near_w = pltpu.roll(own, 1, 2), pltpu.roll(near, 1, 2)
        own_e, near_e = pltpu.roll(own, LANES - 1, 2), pltpu.roll(near, LANES - 1, 2)
        return (
            jnp.where(first_lane, near_w, own_w) + jnp.where(last_lane, near_e, own_e),
            jnp.where(first_lane, own_w, near_w) + jnp.where(last_lane, own_e, near_e),
        )

    def chunks(margin):
        first, last = HALO - margin, HALO + rows + margin
        return [(a, min(a + 8, last)) for a in range(first, last, 8)]

    def smooth_sweep(src, dst, margin, emit=None):
        for a, b in chunks(margin):
            own, near = src[0][a:b], src[1][a:b]
            beside = sides(own, near)
            for ref, value, both, kappa, out in (
                (src[0], own, beside[0], kappa_o, dst[0]),
                (src[1], near, beside[1], kappa_h, dst[1]),
            ):
                if emit is not None and ref is src[1]:
                    continue
                total = ref[a - 1 : b - 1] + ref[a + 1 : b + 1] + both
                value = value + kappa[a:b] * (total - 4.0 * value)
                if emit is None:
                    out[a:b] = value
                else:
                    emit(a, b, value)

    def adjoint_sweep(src, dst, margin, emit=None, near_too=True):
        for a, b in chunks(margin):
            scaled = [
                kappa[a - 1 : b + 1] * ref[a - 1 : b + 1]
                for ref, kappa in ((src[0], kappa_o), (src[1], kappa_h))
            ]
            beside = sides(scaled[0][1:-1], scaled[1][1:-1])
            for which in (0, 1):
                if which and not near_too:
                    continue
                t = scaled[which]
                value = src[which][a:b] + (t[:-2] + t[2:] + beside[which] - 4.0 * t[1:-1])
                if emit is None:
                    dst[which][a:b] = value
                else:
                    emit(which, a, b, value)

    work, following = (work_o, work_h), (next_o, next_h)

    row_waits("alpha", alpha_o, SWEEPS)
    row_waits("kappa", kappa_o, SWEEPS)
    pack_waits("pack", pack_in)
    for e in range(rows + 2 * HALO):
        g, j = divmod(e, GROUP)
        alpha_h[e] = unpacked(lambda peer: pack_in[peer, g, 0], j)
        kappa_h[e] = unpacked(lambda peer: pack_in[peer, g, 1], j)

    for step in range(STEPS):
        term = terms.at[step]

        def emit_term(a, b, value):
            term[a - HALO : b - HALO] = wx_o[a:b] * value

        smooth_sweep((alpha_o, alpha_h), work, SWEEPS - 1)
        src, dst = work, following
        for sweep in range(1, SWEEPS):
            last = sweep == SWEEPS - 1
            smooth_sweep(src, dst, SWEEPS - 1 - sweep, emit_term if last else None)
            src, dst = dst, src

        for hop in range(1, members):
            target = lax.rem(mem + hop, members)
            send(
                None,
                term.at[pl.ds(target * tile_rows, tile_rows)],
                pieces.at[step, hop],
                numbers["sum", step, hop],
                numbers["sum", step, hop],
                device(hop, 0, 0),
            )
        total = term[pl.ds(mem * tile_rows, tile_rows)]
        if step == 0:
            row_waits("kappa_far", kappa_o, HALO - SWEEPS, SWEEPS)
            row_waits("x", wx_o, HALO)
            pack_waits("packx", packx_in)
            for e in range(rows + 2 * HALO):
                g, j = divmod(e, GROUP)
                wx_h[e] = unpacked(lambda peer: packx_in[peer, g], j)
            for side, i, spot in others():
                if side is None:
                    await_in(None, cells_all.at[spot], numbers["cells", i])
                else:
                    await_in(has[side], cells_all.at[spot], numbers["cells_row", side] + i)
            for _, _, spot in others():
                hot(spot, cells_all[spot])
        for hop in range(1, members):
            await_in(None, pieces.at[step, hop], numbers["sum", step, hop])
            total = total + pieces[step, hop]

        flipped = jnp.transpose(total.reshape(spots, LANES))
        hot_rows, hot_cols = rows_hot[mine], cols_hot[mine]
        observed = jnp.zeros((LANES, slots), jnp.float32)
        for half in halves(flipped):
            observed = observed + jnp.dot(half, hot_rows, preferred_element_type=jnp.float32)
        observed = jnp.sum(
            observed * hot_cols.astype(jnp.float32), axis=0, keepdims=True
        )
        misfit = (observed - innovations) * masked_weight
        pulled = jnp.clip(misfit, -huber_edge, huber_edge) * masked_weight
        pulled_out[step] = pulled
        to_group(step, pulled_out.at[step], pulled_in.at[step], ("tile", step))
        tile = spread(mine, pulled)
        edge_out[step] = packed(lambda j: tile[j], tile_rows)

        force_o, edges = forcing_o.at[step], edge_in.at[step]
        for side in (-1, 1):
            near = mem - (0 if side < 0 else members - edge_tiles)
            inside = near < edge_tiles if side < 0 else near >= 0
            condition = jnp.logical_and(has[side], inside)
            spot = near + (edge_tiles + members if side < 0 else 0)
            for peer, lon_hop in enumerate(peers):
                for hop in range(members):
                    send(
                        condition,
                        edge_out.at[step],
                        edges.at[far(peer), spot],
                        numbers["corner_out", step, side, peer] + hop,
                        numbers["corner", step, -side, far(peer)] + near,
                        device(hop, side, lon_hop),
                    )
        for peer, lon_hop in enumerate(peers):
            for hop in range(members):
                send(
                    None,
                    edge_out.at[step],
                    edges.at[far(peer), edge_tiles + mem],
                    numbers["edge", step, peer, hop],
                    numbers["edge", step, far(peer), hop],
                    device(hop, 0, lon_hop),
                )
        force_o[pl.ds(HALO + mem * tile_rows, tile_rows)] = tile

        for side, i, spot in others():
            if side is None:
                await_in(None, pulled_in.at[step, spot], numbers["tile", step, i])
            else:
                await_in(has[side], pulled_in.at[step, spot], numbers["row", step, side] + i)
        for _, _, spot in others():
            force_o[pl.ds(spot * tile_rows, tile_rows)] = spread(spot, pulled_in[step, spot])
        for peer in range(len(peers)):
            for hop in range(members):
                source = lax.rem(mem + members - hop, members)
                await_in(
                    None, edges.at[peer, edge_tiles + source], numbers["edge", step, peer, hop]
                )
        for side in (-1, 1):
            for i in range(edge_tiles):
                spot = i + (0 if side < 0 else edge_tiles + members)
                for peer in range(len(peers)):
                    await_in(
                        has[side],
                        edges.at[peer, spot],
                        numbers["corner", step, side, peer] + i,
                    )

        margin = HALO - step * SWEEPS
        for e in range(HALO - margin, HALO + rows + margin):
            t, j = divmod(e, tile_rows)
            forcing_h[e] = unpacked(lambda peer: edges[peer, t], j)
        for a, b in chunks(margin):
            work_o[a:b] = wx_o[a:b] * force_o[a:b]
            work_h[a:b] = wx_h[a:b] * forcing_h[a:b]

        final = step == STEPS - 1
        inside_top = (lat > 0).astype(jnp.float32)
        inside_bottom = (lat < lat_count - 1).astype(jnp.float32)

        def emit_alpha(which, a, b, value):
            held = (alpha_o, alpha_h)[which]
            old = held[a:b]
            if final:
                fresh = ((1.0 - step_length) / step_length) * old - value
                for r in range(a, b):
                    out_ref[pl.ds(r - HALO, levels, stride=rows), :] = fresh[r - a]
                return
            fresh = old - step_length * (old + value)
            for r in range(a, b):
                row = fresh[r - a]
                if r < HALO:
                    row = row * inside_top
                elif r >= HALO + rows:
                    row = row * inside_bottom
                held[r] = row

        if step == 0:
            settle("alpha")
        src, dst = work, following
        for sweep in range(SWEEPS):
            last = sweep == SWEEPS - 1
            adjoint_sweep(
                src, dst, margin - 1 - sweep, emit_alpha if last else None, not (last and final)
            )
            src, dst = dst, src

    settle()


def fused(members, lat_count, lon_count, tile_rows, x, control, kappa, cells, counts, innov, prec):
    _, levels, rows, columns = x.shape
    peers = 1 if lon_count == 2 else 2
    edge_tiles = HALO // tile_rows
    slots = cells.shape[1]
    groups = rows // GROUP
    _, sent, received = copy_plan(members, peers, edge_tiles)
    vregs = lambda *lead: pltpu.VMEM(lead + (SUBLANES, LANES), jnp.float32)
    deep = rows + 2 * HALO
    tiles = members + 2 * edge_tiles
    vmem = pl.BlockSpec(memory_space=pltpu.VMEM)
    place = pl.BlockSpec(memory_space=pl.ANY)
    flat = lambda dtype: pltpu.VMEM((levels * rows, columns), dtype)
    out = pl.pallas_call(
        functools.partial(kernel, members, lat_count, lon_count, tile_rows),
        out_shape=jax.ShapeDtypeStruct((levels * rows, columns), jnp.float32),
        in_specs=[place] * 4 + [pl.BlockSpec(memory_space=pltpu.SMEM)] + [place] * 2,
        out_specs=vmem,
        scratch_shapes=[
            flat(x.dtype),
            flat(jnp.float32),
            flat(jnp.float32),
            pltpu.VMEM(cells.shape, cells.dtype),
            pltpu.VMEM(innov.shape, innov.dtype),
            pltpu.VMEM(prec.shape, prec.dtype),
            pltpu.SemaphoreType.DMA((6,)),
            flat(jnp.float32),
        ]
        + [vregs(deep)] * 10
        + [
            vregs(STEPS, deep),
            vregs(deep),
            vregs(groups, 2),
            vregs(peers, groups + 2, 2),
            vregs(groups),
            vregs(peers, groups + 2),
            vregs(STEPS),
            vregs(STEPS, peers, tiles),
            vregs(STEPS, rows),
            vregs(STEPS, members, tile_rows),
            pltpu.VMEM((STEPS, 1, slots), jnp.float32),
            pltpu.VMEM((STEPS, tiles, 1, slots), jnp.float32),
            pltpu.VMEM((tiles, 1, slots), jnp.int32),
            pltpu.VMEM((tiles, tile_rows * levels, slots), jnp.bfloat16),
            pltpu.VMEM((tiles, LANES, slots), jnp.bfloat16),
            pltpu.SemaphoreType.DMA((sent,)),
            pltpu.SemaphoreType.DMA((received,)),
        ],
        compiler_params=pltpu.CompilerParams(collective_id=0, has_side_effects=True),
    )(
        x.reshape(levels * rows, columns),
        control.reshape(levels * rows, columns),
        kappa.reshape(levels * rows, columns),
        cells,
        counts,
        innov,
        prec,
    )
    return (step_length * out).reshape(1, levels, rows, columns)


def fits(members, lat_count, lon_count, x, cells):
    _, levels, rows, columns = x.shape
    tile_rows = rows // members
    return (
        levels == SUBLANES
        and columns == LANES
        and rows % members == 0
        and rows % GROUP == 0
        and rows >= 2 * HALO
        and HALO % tile_rows == 0
        and tile_rows <= GROUP
        and HALO // tile_rows <= members
        and lon_count > 1
        and cells.shape[0] == 1
    )


def on_device(members, lat_count, lon_count, x, control, kappa, cells, counts, innov, prec):
    if not fits(members, lat_count, lon_count, x, cells):
        return per_device(x, control, kappa, cells, counts, innov, prec)
    tile_rows = x.shape[2] // members
    return fused(
        members, lat_count, lon_count, tile_rows, x, control, kappa, cells, counts, innov, prec
    )


def solution(mesh):
    return jax.shard_map(
        functools.partial(
            on_device, mesh.shape["mem"], mesh.shape["lat"], mesh.shape["lon"]
        ),
        mesh=mesh,
        in_specs=(
            P("mem", None, "lat", "lon"),
            P("mem", None, "lat", "lon"),
            P(None, "lat", "lon"),
            P(("mem", "lat", "lon"), None),
            P(("mem", "lat", "lon")),
            P(("mem", "lat", "lon"), None),
            P(("mem", "lat", "lon"), None),
        ),
        out_specs=P("mem", None, "lat", "lon"),
        check_vma=False,
    )
```

```python
import functools
import math

import jax
import jax.numpy as jnp
from jax import lax
from jax.experimental import pallas as pl
from jax.experimental.pallas import tpu as pltpu
from jax.sharding import PartitionSpec as P

SWEEPS = 4
STEPS = 2


huber_edge = 1.5
step_length = 0.5


def with_halo(cells, sides, width):
    for axis, dim in sides:
        count = lax.axis_size(axis)
        head = lax.slice_in_dim(cells, 0, width, axis=dim)
        tail = lax.slice_in_dim(cells, cells.shape[dim] - width, cells.shape[dim], axis=dim)
        cells = jnp.concatenate(
            [
                lax.ppermute(tail, axis, [(i, (i + 1) % count) for i in range(count)]),
                cells,
                lax.ppermute(head, axis, [((i + 1) % count, i) for i in range(count)]),
            ],
            axis=dim,
        )
    return cells


def inside_rows(lat_rows, margin):
    first_row = lax.axis_index("lat") * lat_rows - margin
    global_rows = first_row + jnp.arange(lat_rows + 2 * margin, dtype=jnp.int32)
    total_rows = lat_rows * lax.axis_size("lat")
    return ((global_rows >= 0) & (global_rows < total_rows)).astype(jnp.float32)[None, :, None]


def stencil(padded):
    center = padded[:, 1:-1, 1:-1]
    laplace_term = (
        padded[:, :-2, 1:-1]
        + padded[:, 2:, 1:-1]
        + padded[:, 1:-1, :-2]
        + padded[:, 1:-1, 2:]
        - 4.0 * center
    )
    return (laplace_term, center)


def smooth_deep(state_field, kappa_rim):
    lat_rows = state_field.shape[1]
    padded = with_halo(state_field, (("lat", 1), ("lon", 2)), SWEEPS)
    padded = padded * inside_rows(lat_rows, SWEEPS)
    for sweep_index in range(SWEEPS):
        offset = sweep_index + 1
        local_kappa = kappa_rim[
            :, offset : kappa_rim.shape[1] - offset, offset : kappa_rim.shape[2] - offset
        ]
        laplace_term, center = stencil(padded)
        padded = (center + local_kappa * laplace_term) * inside_rows(lat_rows, SWEEPS - offset)
    return padded


def adjoint_deep(state_field, kappa_rim):
    lat_rows = state_field.shape[1]
    padded = with_halo(state_field, (("lat", 1), ("lon", 2)), SWEEPS)
    padded = padded * inside_rows(lat_rows, SWEEPS)
    for sweep_index in range(SWEEPS):
        local_kappa = kappa_rim[
            :,
            sweep_index : kappa_rim.shape[1] - sweep_index,
            sweep_index : kappa_rim.shape[2] - sweep_index,
        ]
        laplace_term, center = stencil(local_kappa * padded)
        padded = (padded[:, 1:-1, 1:-1] + laplace_term) * inside_rows(
            lat_rows, SWEEPS - sweep_index - 1
        )
    return padded


def per_device(
    perturbations, control, diffusivity, obs_cells, obs_counts, innovations, obs_precision
):
    members = lax.axis_size("mem")
    weight = 1.0 / math.sqrt(members - 1)
    member_x = perturbations[0]
    alpha_now = control[0]
    live_slots = (
        jnp.arange(obs_cells.shape[1], dtype=jnp.int32)[None, :] < obs_counts[:, None]
    ).astype(jnp.float32)
    masked_weight = obs_precision * live_slots
    kappa_rim = with_halo(diffusivity, (("lat", 1), ("lon", 2)), SWEEPS)
    for step_index in range(STEPS):
        smoothed = smooth_deep(alpha_now, kappa_rim)
        member_term = member_x.astype(jnp.float32) * smoothed
        owned_piece = lax.psum_scatter(member_term, "mem", scatter_dimension=1, tiled=True)
        increment = weight * owned_piece
        tile_cells = obs_cells[0]
        observed = increment.reshape(-1)[tile_cells]
        misfit = (observed - innovations[0]) * masked_weight[0]
        pulled = jnp.clip(misfit, -huber_edge, huber_edge) * masked_weight[0]
        tile_field = (
            jnp.zeros((increment.size,), jnp.float32)
            .at[tile_cells]
            .add(pulled)
            .reshape(increment.shape)
        )
        forcing = lax.all_gather(tile_field, "mem", axis=1, tiled=True)
        source = weight * member_x.astype(jnp.float32) * forcing
        gradient = alpha_now + adjoint_deep(source, kappa_rim)
        alpha_now = alpha_now - step_length * gradient
    return alpha_now[None]


LANES = 128
SUBLANES = 8
HALO = STEPS * SWEEPS
SLOT = 2 * HALO
GROUP = LANES // SLOT
MESH = pl.DeviceIdType.MESH


def copy_plan(members, peers, edge_tiles):
    keys = []
    for field in ("alpha", "kappa", "kappa_far", "x"):
        keys += [(field, "row", side) for side in (-1, 1)]
    for pack in ("pack", "packx"):
        keys += [(pack, side, peer) for side in (-1, 0, 1) for peer in range(peers)]
    keys += [("cells", hop) for hop in range(1, members)]
    for step in range(STEPS):
        keys += [("sum", step, hop) for hop in range(1, members)]
        keys += [("tile", step, hop) for hop in range(1, members)]
        keys += [("edge", step, peer, hop) for peer in range(peers) for hop in range(members)]
    numbers = {key: number for number, key in enumerate(keys)}
    received = len(keys)
    for side in (-1, 1):
        numbers["cells_row", side] = received
        received += edge_tiles
    for step in range(STEPS):
        for side in (-1, 1):
            numbers["row", step, side] = received
            received += edge_tiles
            for peer in range(peers):
                numbers["corner", step, side, peer] = received
                received += edge_tiles
    sent = len(keys)
    for side in (-1, 1):
        numbers["cells_out", side] = sent
        sent += members
    for step in range(STEPS):
        for side in (-1, 1):
            numbers["row_out", step, side] = sent
            sent += members
            for peer in range(peers):
                numbers["corner_out", step, side, peer] = sent
                sent += members
    return numbers, sent, received


def kernel(
    members,
    lat_count,
    lon_count,
    tile_rows,
    x_in,
    control_in,
    kappa_in,
    cells_in,
    counts_ref,
    innovations_in,
    precision_in,
    out_ref,
    x_ref,
    control_ref,
    kappa_ref,
    cells_ref,
    innovations_ref,
    precision_ref,
    load_sems,
    x_flat,
    alpha_o,
    alpha_h,
    kappa_o,
    kappa_h,
    wx_o,
    wx_h,
    work_o,
    work_h,
    next_o,
    next_h,
    forcing_o,
    forcing_h,
    pack_out,
    pack_in,
    packx_out,
    packx_in,
    edge_out,
    edge_in,
    terms,
    pieces,
    pulled_out,
    pulled_in,
    cells_all,
    rows_hot,
    cols_hot,
    send_sems,
    recv_sems,
):
    levels = SUBLANES
    rows = control_ref.shape[0] // levels
    slots = cells_ref.shape[1]
    groups = rows // GROUP
    edge_tiles = HALO // tile_rows
    peers = [1] if lon_count == 2 else [1, lon_count - 1]
    numbers, _, _ = copy_plan(members, len(peers), edge_tiles)
    weight = 1.0 / math.sqrt(members - 1)
    mem = lax.axis_index("mem")
    lat = lax.axis_index("lat")
    lon = lax.axis_index("lon")
    has = {-1: lat > 0, 0: None, 1: lat < lat_count - 1}

    def guarded(condition, run):
        if condition is None:
            run()
        else:
            pl.when(condition)(run)

    def device(mem_hop, lat_hop, lon_hop):
        return (
            lax.rem(mem + mem_hop, members),
            lat + lat_hop,
            lax.rem(lon + lon_hop, lon_count),
        )

    def far(peer):
        return len(peers) - 1 - peer

    def remote(src, dst, send_number, recv_number, target):
        return pltpu.make_async_remote_copy(
            src_ref=src,
            dst_ref=dst,
            send_sem=send_sems.at[send_number],
            recv_sem=recv_sems.at[recv_number],
            device_id=target,
            device_id_type=MESH,
        )

    pending = []

    def send(condition, src, dst, send_number, recv_number, target):
        guarded(condition, lambda: remote(src, dst, send_number, recv_number, target).start())
        pending.append((condition, src, send_number))

    def settle(name=None):
        kept = []
        for condition, src, number in pending:
            if name is None or number in (numbers[name, "row", -1], numbers[name, "row", 1]):
                guarded(
                    condition,
                    lambda: remote(src, src, number, 0, device(0, 0, peers[0])).wait_send(),
                )
            else:
                kept.append((condition, src, number))
        pending[:] = kept

    def await_in(condition, dst, recv_number):
        guarded(
            condition,
            lambda: remote(dst, dst, 0, recv_number, device(0, 0, peers[0])).wait_recv(),
        )

    loads = [
        pltpu.make_async_copy(src, dst, load_sems.at[number])
        for number, (src, dst) in enumerate(
            (
                (control_in, control_ref),
                (kappa_in, kappa_ref),
                (x_in, x_ref),
                (cells_in, cells_ref),
                (innovations_in, innovations_ref),
                (precision_in, precision_ref),
            )
        )
    ]
    for load in loads:
        load.start()

    barrier = pltpu.get_barrier_semaphore()
    for lat_hop in (0, -1, 1):
        def greet(lat_hop=lat_hop):
            for lon_hop in [0] + peers:
                for mem_hop in range(members if lon_hop == 0 else 1):
                    if (lat_hop, lon_hop, mem_hop) != (0, 0, 0):
                        pl.semaphore_signal(
                            barrier,
                            inc=1,
                            device_id=device(mem_hop, lat_hop, lon_hop),
                            device_id_type=MESH,
                        )
        guarded(has[lat_hop], greet)

    lane = lax.broadcasted_iota(jnp.int32, (1, SUBLANES, LANES), 2)
    lane2 = lane[0]

    for load in loads:
        load.wait()
    x_flat[...] = weight * x_ref[...].astype(jnp.float32)
    for r in range(rows):
        level_rows = pl.ds(r, levels, stride=rows)
        alpha_o[HALO + r] = control_ref[level_rows, :]
        kappa_o[HALO + r] = kappa_ref[level_rows, :]
        wx_o[HALO + r] = x_flat[level_rows, :]

    def packed(read, count):
        total = jnp.zeros((SUBLANES, LANES), jnp.float32)
        for j in range(count):
            shifted = pltpu.roll(read(j), (HALO + SLOT * j) % LANES, 1)
            total = jnp.where(lane2 // SLOT == j, shifted, total)
        return total

    def unpacked(read, j):
        shift = (LANES - HALO - SLOT * j) % LANES
        parts = [pltpu.roll(read(peer), shift, 1) if shift else read(peer) for peer in range(len(peers))]
        if len(parts) == 1:
            return parts[0]
        return jnp.where(lane2 < LANES // 2, parts[0], parts[1])

    for g in range(groups):
        base = HALO + g * GROUP
        pack_out[g, 0] = packed(lambda j: alpha_o[base + j], GROUP)
        pack_out[g, 1] = packed(lambda j: kappa_o[base + j], GROUP)
        packx_out[g] = packed(lambda j: wx_o[base + j], GROUP)

    zero_rows = jnp.zeros((HALO, SUBLANES, LANES), jnp.float32)
    for side in (-1, 1):
        start = 0 if side < 0 else HALO + rows
        group = 0 if side < 0 else groups + 1
        tile = 0 if side < 0 else edge_tiles + members

        def clear(start=start, group=group, tile=tile):
            for ref in (alpha_o, kappa_o, wx_o):
                ref[start : start + HALO] = zero_rows
            cells_all[tile : tile + edge_tiles] = jnp.zeros((edge_tiles, 1, slots), jnp.int32)
            for step in range(STEPS):
                pulled_in[step, tile : tile + edge_tiles] = jnp.zeros(
                    (edge_tiles, 1, slots), jnp.float32
                )
            for peer in range(len(peers)):
                pack_in[peer, group] = jnp.zeros((2, SUBLANES, LANES), jnp.float32)
                packx_in[peer, group] = jnp.zeros((SUBLANES, LANES), jnp.float32)
                for step in range(STEPS):
                    edge_in[step, peer, tile : tile + edge_tiles] = jnp.zeros(
                        (edge_tiles, SUBLANES, LANES), jnp.float32
                    )

        guarded(jnp.logical_not(has[side]), clear)

    greeted = len(peers) + members
    lat_near = 1 + (lat > 0).astype(jnp.int32) + (lat < lat_count - 1).astype(jnp.int32)
    pl.semaphore_wait(barrier, greeted * lat_near - 1)

    def row_copies(name, field, width, skip=0):
        for side in (-1, 1):
            source = HALO + skip if side < 0 else HALO + rows - width - skip
            target = HALO + rows + skip if side < 0 else HALO - width - skip
            send(
                has[side],
                field.at[pl.ds(source, width)],
                field.at[pl.ds(target, width)],
                numbers[name, "row", side],
                numbers[name, "row", -side],
                device(0, side, 0),
            )

    def row_waits(name, field, width, skip=0):
        for side in (-1, 1):
            start = HALO - width - skip if side < 0 else HALO + rows + skip
            await_in(has[side], field.at[pl.ds(start, width)], numbers[name, "row", side])

    def pack_copies(name, source, target):
        for side in (0, -1, 1):
            for peer, hop in enumerate(peers):
                if side == 0:
                    src, dst = source, target.at[far(peer), pl.ds(1, groups)]
                elif side < 0:
                    src, dst = source.at[0], target.at[far(peer), groups + 1]
                else:
                    src, dst = source.at[groups - 1], target.at[far(peer), 0]
                send(
                    has[side],
                    src,
                    dst,
                    numbers[name, side, peer],
                    numbers[name, -side, far(peer)],
                    device(0, side, hop),
                )

    def pack_waits(name, target):
        for side in (0, -1, 1):
            for peer in range(len(peers)):
                if side == 0:
                    dst = target.at[peer, pl.ds(1, groups)]
                else:
                    dst = target.at[peer, 0 if side < 0 else groups + 1]
                await_in(has[side], dst, numbers[name, side, peer])

    pack_copies("pack", pack_out, pack_in)
    row_copies("alpha", alpha_o, SWEEPS)
    row_copies("kappa", kappa_o, SWEEPS)
    pack_copies("packx", packx_out, packx_in)
    row_copies("kappa_far", kappa_o, HALO - SWEEPS, SWEEPS)
    row_copies("x", wx_o, HALO)

    def to_group(step, source, target, name):
        for hop in range(1, members):
            send(
                None,
                source,
                target.at[edge_tiles + mem],
                numbers[name + (hop,)],
                numbers[name + (hop,)],
                device(hop, 0, 0),
            )
        outs, ins = ("cells_out", "cells_row") if step is None else ("row_out", "row")
        key = () if step is None else (step,)
        for side in (-1, 1):
            near = mem - (0 if side < 0 else members - edge_tiles)
            inside = near < edge_tiles if side < 0 else near >= 0
            for hop in range(members):
                send(
                    jnp.logical_and(has[side], inside),
                    source,
                    target.at[near + (edge_tiles + members if side < 0 else 0)],
                    numbers[(outs,) + key + (side,)] + hop,
                    numbers[(ins,) + key + (-side,)] + near,
                    device(hop, side, 0),
                )

    def others():
        for hop in range(1, members):
            yield None, hop, edge_tiles + lax.rem(mem + members - hop, members)
        for side in (-1, 1):
            for i in range(edge_tiles):
                yield side, i, i + (0 if side < 0 else edge_tiles + members)

    to_group(None, cells_ref, cells_all, ("cells",))

    spots = tile_rows * levels

    def hot(spot, cells):
        column = lax.rem(cells, LANES)
        tile_row = lax.rem(lax.div(cells, LANES), tile_rows)
        level = lax.div(cells, LANES * tile_rows)
        place = tile_row * levels + level
        rows_hot[spot] = (
            lax.broadcasted_iota(jnp.int32, (spots, slots), 0) == place
        ).astype(jnp.float32).astype(jnp.bfloat16)
        cols_hot[spot] = (
            lax.broadcasted_iota(jnp.int32, (LANES, slots), 0) == column
        ).astype(jnp.float32).astype(jnp.bfloat16)

    def spread(spot, pulled):
        tile = jnp.zeros((spots, LANES), jnp.float32)
        for half in halves(pulled):
            tile = tile + lax.dot_general(
                rows_hot[spot] * half,
                cols_hot[spot],
                (((1,), (1,)), ((), ())),
                preferred_element_type=jnp.float32,
            )
        return tile.reshape(tile_rows, SUBLANES, LANES)

    mine = edge_tiles + mem
    hot(mine, cells_ref[...])
    live = (
        lax.broadcasted_iota(jnp.int32, (1, slots), 1) < counts_ref[0]
    ).astype(jnp.float32)
    masked_weight = precision_ref[...] * live
    innovations = innovations_ref[...]

    def halves(value):
        high = value.astype(jnp.bfloat16)
        return high, (value - high.astype(jnp.float32)).astype(jnp.bfloat16)

    first_lane, last_lane = lane == 0, lane == LANES - 1

    def sides(own, near):
        own_w, near_w = pltpu.roll(own, 1, 2), pltpu.roll(near, 1, 2)
        own_e, near_e = pltpu.roll(own, LANES - 1, 2), pltpu.roll(near, LANES - 1, 2)
        return (
            jnp.where(first_lane, near_w, own_w) + jnp.where(last_lane, near_e, own_e),
            jnp.where(first_lane, own_w, near_w) + jnp.where(last_lane, own_e, near_e),
        )

    def chunks(margin):
        first, last = HALO - margin, HALO + rows + margin
        return [(a, min(a + 8, last)) for a in range(first, last, 8)]

    def smooth_sweep(src, dst, margin, emit=None):
        for a, b in chunks(margin):
            own, near = src[0][a:b], src[1][a:b]
            beside = sides(own, near)
            for ref, value, both, kappa, out in (
                (src[0], own, beside[0], kappa_o, dst[0]),
                (src[1], near, beside[1], kappa_h, dst[1]),
            ):
                if emit is not None and ref is src[1]:
                    continue
                total = ref[a - 1 : b - 1] + ref[a + 1 : b + 1] + both
                value = value + kappa[a:b] * (total - 4.0 * value)
                if emit is None:
                    out[a:b] = value
                else:
                    emit(a, b, value)

    def adjoint_sweep(src, dst, margin, emit=None, near_too=True):
        for a, b in chunks(margin):
            scaled = [
                kappa[a - 1 : b + 1] * ref[a - 1 : b + 1]
                for ref, kappa in ((src[0], kappa_o), (src[1], kappa_h))
            ]
            beside = sides(scaled[0][1:-1], scaled[1][1:-1])
            for which in (0, 1):
                if which and not near_too:
                    continue
                t = scaled[which]
                value = src[which][a:b] + (t[:-2] + t[2:] + beside[which] - 4.0 * t[1:-1])
                if emit is None:
                    dst[which][a:b] = value
                else:
                    emit(which, a, b, value)

    work, following = (work_o, work_h), (next_o, next_h)

    row_waits("alpha", alpha_o, SWEEPS)
    row_waits("kappa", kappa_o, SWEEPS)
    pack_waits("pack", pack_in)
    for e in range(rows + 2 * HALO):
        g, j = divmod(e, GROUP)
        alpha_h[e] = unpacked(lambda peer: pack_in[peer, g, 0], j)
        kappa_h[e] = unpacked(lambda peer: pack_in[peer, g, 1], j)

    for step in range(STEPS):
        term = terms.at[step]

        def emit_term(a, b, value):
            term[a - HALO : b - HALO] = wx_o[a:b] * value

        smooth_sweep((alpha_o, alpha_h), work, SWEEPS - 1)
        src, dst = work, following
        for sweep in range(1, SWEEPS):
            last = sweep == SWEEPS - 1
            smooth_sweep(src, dst, SWEEPS - 1 - sweep, emit_term if last else None)
            src, dst = dst, src

        for hop in range(1, members):
            target = lax.rem(mem + hop, members)
            send(
                None,
                term.at[pl.ds(target * tile_rows, tile_rows)],
                pieces.at[step, hop],
                numbers["sum", step, hop],
                numbers["sum", step, hop],
                device(hop, 0, 0),
            )
        total = term[pl.ds(mem * tile_rows, tile_rows)]
        if step == 0:
            row_waits("kappa_far", kappa_o, HALO - SWEEPS, SWEEPS)
            row_waits("x", wx_o, HALO)
            pack_waits("packx", packx_in)
            for e in range(rows + 2 * HALO):
                g, j = divmod(e, GROUP)
                wx_h[e] = unpacked(lambda peer: packx_in[peer, g], j)
            for side, i, spot in others():
                if side is None:
                    await_in(None, cells_all.at[spot], numbers["cells", i])
                else:
                    await_in(has[side], cells_all.at[spot], numbers["cells_row", side] + i)
            for _, _, spot in others():
                hot(spot, cells_all[spot])
        for hop in range(1, members):
            await_in(None, pieces.at[step, hop], numbers["sum", step, hop])
            total = total + pieces[step, hop]

        flipped = jnp.transpose(total.reshape(spots, LANES))
        hot_rows, hot_cols = rows_hot[mine], cols_hot[mine]
        observed = jnp.zeros((LANES, slots), jnp.float32)
        for half in halves(flipped):
            observed = observed + jnp.dot(half, hot_rows, preferred_element_type=jnp.float32)
        observed = jnp.sum(
            observed * hot_cols.astype(jnp.float32), axis=0, keepdims=True
        )
        misfit = (observed - innovations) * masked_weight
        pulled = jnp.clip(misfit, -huber_edge, huber_edge) * masked_weight
        pulled_out[step] = pulled
        to_group(step, pulled_out.at[step], pulled_in.at[step], ("tile", step))
        tile = spread(mine, pulled)
        edge_out[step] = packed(lambda j: tile[j], tile_rows)

        force_o, edges = forcing_o.at[step], edge_in.at[step]
        for side in (-1, 1):
            near = mem - (0 if side < 0 else members - edge_tiles)
            inside = near < edge_tiles if side < 0 else near >= 0
            condition = jnp.logical_and(has[side], inside)
            spot = near + (edge_tiles + members if side < 0 else 0)
            for peer, lon_hop in enumerate(peers):
                for hop in range(members):
                    send(
                        condition,
                        edge_out.at[step],
                        edges.at[far(peer), spot],
                        numbers["corner_out", step, side, peer] + hop,
                        numbers["corner", step, -side, far(peer)] + near,
                        device(hop, side, lon_hop),
                    )
        for peer, lon_hop in enumerate(peers):
            for hop in range(members):
                send(
                    None,
                    edge_out.at[step],
                    edges.at[far(peer), edge_tiles + mem],
                    numbers["edge", step, peer, hop],
                    numbers["edge", step, far(peer), hop],
                    device(hop, 0, lon_hop),
                )
        force_o[pl.ds(HALO + mem * tile_rows, tile_rows)] = tile

        for side, i, spot in others():
            if side is None:
                await_in(None, pulled_in.at[step, spot], numbers["tile", step, i])
            else:
                await_in(has[side], pulled_in.at[step, spot], numbers["row", step, side] + i)
        for _, _, spot in others():
            force_o[pl.ds(spot * tile_rows, tile_rows)] = spread(spot, pulled_in[step, spot])
        for peer in range(len(peers)):
            for hop in range(members):
                source = lax.rem(mem + members - hop, members)
                await_in(
                    None, edges.at[peer, edge_tiles + source], numbers["edge", step, peer, hop]
                )
        for side in (-1, 1):
            for i in range(edge_tiles):
                spot = i + (0 if side < 0 else edge_tiles + members)
                for peer in range(len(peers)):
                    await_in(
                        has[side],
                        edges.at[peer, spot],
                        numbers["corner", step, side, peer] + i,
                    )

        margin = HALO - step * SWEEPS
        for e in range(HALO - margin, HALO + rows + margin):
            t, j = divmod(e, tile_rows)
            forcing_h[e] = unpacked(lambda peer: edges[peer, t], j)
        for a, b in chunks(margin):
            work_o[a:b] = wx_o[a:b] * force_o[a:b]
            work_h[a:b] = wx_h[a:b] * forcing_h[a:b]

        final = step == STEPS - 1
        inside_top = (lat > 0).astype(jnp.float32)
        inside_bottom = (lat < lat_count - 1).astype(jnp.float32)

        def emit_alpha(which, a, b, value):
            held = (alpha_o, alpha_h)[which]
            old = held[a:b]
            if final:
                fresh = ((1.0 - step_length) / step_length) * old - value
                for r in range(a, b):
                    out_ref[pl.ds(r - HALO, levels, stride=rows), :] = fresh[r - a]
                return
            fresh = old - step_length * (old + value)
            for r in range(a, b):
                row = fresh[r - a]
                if r < HALO:
                    row = row * inside_top
                elif r >= HALO + rows:
                    row = row * inside_bottom
                held[r] = row

        if step == 0:
            settle("alpha")
        src, dst = work, following
        for sweep in range(SWEEPS):
            last = sweep == SWEEPS - 1
            adjoint_sweep(
                src, dst, margin - 1 - sweep, emit_alpha if last else None, not (last and final)
            )
            src, dst = dst, src

    settle()


def fused(members, lat_count, lon_count, tile_rows, x, control, kappa, cells, counts, innov, prec):
    _, levels, rows, columns = x.shape
    peers = 1 if lon_count == 2 else 2
    edge_tiles = HALO // tile_rows
    slots = cells.shape[1]
    groups = rows // GROUP
    _, sent, received = copy_plan(members, peers, edge_tiles)
    vregs = lambda *lead: pltpu.VMEM(lead + (SUBLANES, LANES), jnp.float32)
    deep = rows + 2 * HALO
    tiles = members + 2 * edge_tiles
    vmem = pl.BlockSpec(memory_space=pltpu.VMEM)
    place = pl.BlockSpec(memory_space=pl.ANY)
    flat = lambda dtype: pltpu.VMEM((levels * rows, columns), dtype)
    out = pl.pallas_call(
        functools.partial(kernel, members, lat_count, lon_count, tile_rows),
        out_shape=jax.ShapeDtypeStruct((levels * rows, columns), jnp.float32),
        in_specs=[place] * 4 + [pl.BlockSpec(memory_space=pltpu.SMEM)] + [place] * 2,
        out_specs=vmem,
        scratch_shapes=[
            flat(x.dtype),
            flat(jnp.float32),
            flat(jnp.float32),
            pltpu.VMEM(cells.shape, cells.dtype),
            pltpu.VMEM(innov.shape, innov.dtype),
            pltpu.VMEM(prec.shape, prec.dtype),
            pltpu.SemaphoreType.DMA((6,)),
            flat(jnp.float32),
        ]
        + [vregs(deep)] * 10
        + [
            vregs(STEPS, deep),
            vregs(deep),
            vregs(groups, 2),
            vregs(peers, groups + 2, 2),
            vregs(groups),
            vregs(peers, groups + 2),
            vregs(STEPS),
            vregs(STEPS, peers, tiles),
            vregs(STEPS, rows),
            vregs(STEPS, members, tile_rows),
            pltpu.VMEM((STEPS, 1, slots), jnp.float32),
            pltpu.VMEM((STEPS, tiles, 1, slots), jnp.float32),
            pltpu.VMEM((tiles, 1, slots), jnp.int32),
            pltpu.VMEM((tiles, tile_rows * levels, slots), jnp.bfloat16),
            pltpu.VMEM((tiles, LANES, slots), jnp.bfloat16),
            pltpu.SemaphoreType.DMA((sent,)),
            pltpu.SemaphoreType.DMA((received,)),
        ],
        compiler_params=pltpu.CompilerParams(collective_id=0, has_side_effects=True),
    )(
        x.reshape(levels * rows, columns),
        control.reshape(levels * rows, columns),
        kappa.reshape(levels * rows, columns),
        cells,
        counts,
        innov,
        prec,
    )
    return (step_length * out).reshape(1, levels, rows, columns)


def fits(members, lat_count, lon_count, x, cells):
    _, levels, rows, columns = x.shape
    tile_rows = rows // members
    return (
        levels == SUBLANES
        and columns == LANES
        and rows % members == 0
        and rows % GROUP == 0
        and rows >= 2 * HALO
        and HALO % tile_rows == 0
        and tile_rows <= GROUP
        and HALO // tile_rows <= members
        and lon_count > 1
        and cells.shape[0] == 1
    )


def on_device(members, lat_count, lon_count, x, control, kappa, cells, counts, innov, prec):
    if not fits(members, lat_count, lon_count, x, cells):
        return per_device(x, control, kappa, cells, counts, innov, prec)
    tile_rows = x.shape[2] // members
    return fused(
        members, lat_count, lon_count, tile_rows, x, control, kappa, cells, counts, innov, prec
    )


def solution(mesh):
    return jax.shard_map(
        functools.partial(
            on_device, mesh.shape["mem"], mesh.shape["lat"], mesh.shape["lon"]
        ),
        mesh=mesh,
        in_specs=(
            P("mem", None, "lat", "lon"),
            P("mem", None, "lat", "lon"),
            P(None, "lat", "lon"),
            P(("mem", "lat", "lon"), None),
            P(("mem", "lat", "lon")),
            P(("mem", "lat", "lon"), None),
            P(("mem", "lat", "lon"), None),
        ),
        out_specs=P("mem", None, "lat", "lon"),
        check_vma=False,
    )
```
